256 devices in a mesh: dp: 32 (over y, z), head: 4 (over x), rep: 2 (over core).
Axes of the slice: x: 4, y: 4, z: 8, core: 2. Of those that a mesh axis runs over, the one named last changes fastest.
Arguments:
- embeddings: bfloat16 [16384, 8, 1152], P(('dp', 'head', 'rep')), may hold values from -6 to 6
- coverage: int32 [16384, 2], P(('dp', 'head', 'rep')), may hold values from 0 to 127, all different within a row; in each aligned block of 64 rows (0 to 63, 64 to 127, ...) at most 2 rows name the same one
- labels: int32 [16384, 2, 8], P(('dp', 'head', 'rep')), may hold values 0 or 1
- w_in: bfloat16 [128, 1152, 768], P(('dp', 'head')), may hold values from -0.1875 to 0.1875
- bias_in: bfloat16 [128, 768], P(('dp', 'head')), may hold values from -3 to 3
- w_out: bfloat16 [128, 768], P(('dp', 'head')), may hold values from -0.21875 to 0.21875
- first_w: float32 [128, 1152, 768], P(('dp', 'head'), 'rep'), may hold values from -0.5 to 0.5
- second_w: float32 [128, 1152, 768], P(('dp', 'head'), 'rep'), may hold values from 0.0001 to 0.001
- first_vec: float32 [128, 2, 768], P(('dp', 'head')), may hold values from -0.5 to 0.5
- second_vec: float32 [128, 2, 768], P(('dp', 'head')), may hold values from 0.0001 to 0.01
Outputs:
- new_w_in: bfloat16 [128, 1152, 768], P(('dp', 'head'))
- new_vec: bfloat16 [128, 2, 768], P(('dp', 'head'))
- new_first_w: float32 [128, 1152, 768], P(('dp', 'head'), 'rep')
- new_second_w: float32 [128, 1152, 768], P(('dp', 'head'), 'rep')
- new_first_vec: float32 [128, 2, 768], P(('dp', 'head'))
- new_second_vec: float32 [128, 2, 768], P(('dp', 'head'))
The draws below stay inside these ranges and needn't reach their ends.
Inputs may be any that keep to these rules, and one draw needn't show every extreme that they name: `coverage`: each block names 2 different heads. Among the 64 blocks of one device (aligned blocks of rows, in order) no head is named more than 2 times, a bound that some block reaches; every head is named by some block.
All inputs are finite; a program needn't handle non-finite values. No bound on the sum of `labels` on one device may be relied on, other than what follows from the above.
Results may differ from the reference program's by a relative error of at most 0.00155.
Values may be sent and summed in bfloat16 or wider, within the bound.
A program may use at most 128 MiB of HBM per device.

```python
import math
import jax
import jax.numpy as jnp
import numpy as np
from jax import lax

D = 1152
HID = 768
ROWS_BLK = 8
TOP = 2
BLK_DEV = 64
HEADS = 128
MOST = 2
BLOCKS = 16384
N_DP = 32
N_HEAD = 4
N_REP = 2


def set_ends(array, stream_key, low, largest):
    longest = array.shape.index(max(array.shape))
    spots = []
    for shift in (0, 1):
        where = [jax.random.randint(jax.random.fold_in(stream_key, axis), (), 0, length) for axis, length in enumerate(array.shape)]
        where[longest] = (where[longest] + shift) % array.shape[longest]
        spots.append(tuple(where))
    return array.at[spots[0]].set(low).at[spots[1]].set(largest)


def steps_of(own_key, dims, shards, least, largest):
    loudness, own = 1.0, jax.random.fold_in(own_key, 6)
    for axis_at, shards_of in shards:
        heights = jnp.exp(jax.random.uniform(jax.random.fold_in(own, axis_at), (shards_of,), jnp.float32, least / len(shards), largest / len(shards)))
        loudness = loudness * jnp.repeat(heights, dims[axis_at] // shards_of).reshape([-1 if axis == axis_at else 1 for axis in range(len(dims))])
    return loudness


def shared_out(rng, own, number, rows, number_of, top, most, slope):
    order = jax.random.permutation(rng, number_of)
    heavy_load, common = portions_of(number_of, rows * top, most, slope, True), portions_of(number_of, rows * top, most, slope, False)
    places = jnp.arange(number_of)

    def named(sizes, turn):
        used = int((sizes > 0).sum())
        fixed = max(1, used // 4)
        shifted = fixed + (places - fixed + turn * (used - fixed)) % max(1, number_of - fixed)
        return jnp.zeros((number_of,), jnp.int32).at[order[jnp.where(places < fixed, places, shifted)]].set(jnp.asarray(sizes, jnp.int32))

    sizes = jnp.where(number % 4 == 0, named(heavy_load, number // 4), named(common, number - number // 4 - 1))
    mixed = jax.random.permutation(jax.random.fold_in(own, 3), number_of)
    donor, receiver = mixed[0:number_of // 2 * 2:2], mixed[1:number_of // 2 * 2:2]
    room = jnp.minimum(sizes[donor] - 1, most - sizes[receiver]) // 2
    room = jnp.where((donor == order[0]) | (receiver == order[0]) | (sizes[receiver] == 0), 0, jnp.maximum(room, 0))
    shifted = jax.random.randint(jax.random.fold_in(own, 4), (number_of // 2,), 0, 1 << 20) % (room + 1)
    sizes = sizes.at[donor].add(-shifted).at[receiver].add(shifted)
    members = jnp.searchsorted(jnp.cumsum(sizes), jnp.arange(rows * top), side="right").astype(jnp.int32)
    listing = members.reshape(top, rows).T
    listing = listing[jax.random.permutation(jax.random.fold_in(own, 1), rows)]
    turn = jax.random.randint(jax.random.fold_in(own, 2), (rows, 1), 0, top)
    return jnp.take_along_axis(listing, (jnp.arange(top)[None, :] + turn) % top, axis=1)


def portions_of(number_of, total, reach, skew, full):
    weights = [(1 << 20) // math.isqrt(standing ** skew) + 1 for standing in range(1, number_of + 1)]
    largest = reach if full else min(reach, max(-(-total // number_of), total * weights[0] // sum(weights)))
    least = 1 if total - largest >= number_of - 1 else 0
    given, rest = [largest] + [least] * (number_of - 1), total - largest - least * (number_of - 1)
    while rest > 0:
        movable = [i for i in range(1, number_of) if given[i] < largest] or [i for i in range(1, number_of) if given[i] < reach]
        whole, budget = sum([weights[i] for i in movable]), rest
        for i in movable:
            extra = min(reach - given[i], max(1, budget * weights[i] // whole), rest)
            given[i] = given[i] + extra
            rest = rest - extra
    return np.array(given)


def scatter_about(key, shape, spread, bound, split=(), kind=jnp.bfloat16):
    values = spread * jax.random.normal(key, shape, jnp.float32)
    if split:
        values = values * steps_of(key, shape, split, -0.22, 0.18)
    return jnp.clip(values, -bound, bound).astype(kind)


def setup_inputs(seed: int = 0) -> dict:
    key_of = jax.random.split(jax.random.key(seed), 11)
    embeddings = scatter_about(key_of[0], (BLOCKS, ROWS_BLK, D), 1.0, 6.0, ((0, 256),))
    coverage_keys = jax.random.split(jax.random.fold_in(key_of[1], 1), BLOCKS // BLK_DEV)
    coverage_turns = jax.random.permutation(jax.random.fold_in(key_of[1], 3), BLOCKS // BLK_DEV)
    coverage = jax.vmap(lambda own, number: shared_out(jax.random.fold_in(key_of[1], 2), own, number, BLK_DEV, HEADS, TOP, MOST, 2))(coverage_keys, coverage_turns).reshape((BLOCKS, TOP))
    labels = set_ends((jax.random.randint(key_of[2], (BLOCKS, TOP, ROWS_BLK), 0, 2) < 1).astype(jnp.int32), jax.random.fold_in(key_of[2], 1), 0, 1)
    w_in = scatter_about(key_of[3], (HEADS, D, HID), D ** -0.5, 0.1875, ((0, 128),))
    bias_in = scatter_about(key_of[4], (HEADS, HID), 0.5, 3.0, ((0, 128),))
    w_out = scatter_about(key_of[5], (HEADS, HID), HID ** -0.5, 0.21875, ((0, 128),))
    first_w = scatter_about(key_of[6], (HEADS, D, HID), 0.1, 0.5, ((0, 128), (1, 2)), jnp.float32)
    second_w = jnp.clip(jnp.exp(math.log(0.001) - 2.3025852 * jax.random.uniform(key_of[7], (HEADS, D, HID), jnp.float32) ** steps_of(key_of[7], (HEADS, D, HID), ((0, 128), (1, 2)), -0.2, 0.2)), 0.0001, 0.001)
    first_vec = scatter_about(key_of[8], (HEADS, 2, HID), 0.1, 0.5, ((0, 128),), jnp.float32)
    second_vec = jnp.clip(jnp.exp(math.log(0.01) - 4.6051702 * jax.random.uniform(key_of[9], (HEADS, 2, HID), jnp.float32) ** steps_of(key_of[9], (HEADS, 2, HID), ((0, 128),), -0.2, 0.2)), 0.0001, 0.01)
    return {"embeddings": embeddings, "coverage": coverage, "labels": labels, "w_in": w_in, "bias_in": bias_in, "w_out": w_out, "first_w": first_w, "second_w": second_w, "first_vec": first_vec, "second_vec": second_vec}


beta_one = 0.9
beta_two = 0.999
learn_rate = 0.001
epsilon = 1e-08

def reference(embeddings, coverage, labels, w_in, bias_in, w_out, first_w, second_w, first_vec, second_vec):
    entry_bound = N_DP * N_HEAD * N_REP * MOST
    heads_flat = coverage.reshape(-1)
    targets_all = labels.reshape(-1, ROWS_BLK)

    def one_head(head_id):
        entry_order = jnp.argsort((heads_flat != head_id).astype(jnp.int32), stable=True)[:entry_bound].astype(jnp.int32)
        usable = heads_flat[entry_order] == head_id
        block_ids = (entry_order // TOP).astype(jnp.int32)
        row_data = embeddings[block_ids].reshape(entry_bound * ROWS_BLK, D)
        target = targets_all[entry_order].reshape(-1).astype(jnp.float32)
        row_keep = jnp.repeat(usable, ROWS_BLK)
        out_weight = w_out[head_id].astype(jnp.float32)
        pre_act = jnp.dot(row_data, w_in[head_id], preferred_element_type=jnp.float32) + bias_in[head_id].astype(jnp.float32)
        sig_pre = jax.nn.sigmoid(pre_act)
        hidden = pre_act * sig_pre
        logits = lax.optimization_barrier(jnp.sum(hidden * out_weight[None, :], axis=1))
        residual = jnp.where(row_keep, jax.nn.sigmoid(logits) - target, jnp.zeros_like(logits))
        grad_pre = residual[:, None] * out_weight[None, :] * sig_pre * (1.0 + pre_act * (1.0 - sig_pre))
        grad_low = grad_pre.astype(jnp.bfloat16)
        grad_w = lax.dot_general(row_data, grad_low, (((0,), (0,)), ((), ())), preferred_element_type=jnp.float32)
        grad_vec = jnp.stack([lax.optimization_barrier(jnp.sum(grad_pre, axis=0)), lax.optimization_barrier(jnp.sum(residual[:, None] * hidden, axis=0))])
        return (grad_w, grad_vec)
    grad_w, grad_vec = lax.map(one_head, jnp.arange(HEADS, dtype=jnp.int32))
    new_first_w = beta_one * first_w + (1.0 - beta_one) * grad_w
    new_second_w = beta_two * second_w + (1.0 - beta_two) * grad_w * grad_w
    new_w_in = (w_in.astype(jnp.float32) - learn_rate * new_first_w / (jnp.sqrt(new_second_w) + epsilon)).astype(jnp.bfloat16)
    vector = jnp.stack([bias_in, w_out], axis=1).astype(jnp.float32)
    new_first_vec = beta_one * first_vec + (1.0 - beta_one) * grad_vec
    new_second_vec = beta_two * second_vec + (1.0 - beta_two) * grad_vec * grad_vec
    new_vec = (vector - learn_rate * new_first_vec / (jnp.sqrt(new_second_vec) + epsilon)).astype(jnp.bfloat16)
    return (new_w_in, new_vec, new_first_w, new_second_w, new_first_vec, new_second_vec)
```

```python
import jax
import jax.numpy as jnp
from jax import lax
from jax.experimental import pallas as pl
from jax.experimental.pallas import tpu as pltpu
from jax.sharding import PartitionSpec as P

beta_one = 0.9
beta_two = 0.999
learn_rate = 0.001
epsilon = 1e-08

MESH = pl.DeviceIdType.MESH
NZ = 8
STEP_OF = (0, 1, 3, 5, 7, 6, 4, 2)
CUTS = ((0, 16), (16, 48), (48, 64))
CUTS_AT = {1: 3, 2: 3, 3: 2, 4: 1}
HOP_SIZE = (64, 64, 48, 16)


def plan(coverage, labels, z):
    blocks, top = coverage.shape
    rows = labels.shape[2]
    head = coverage
    plane = (head // 4) % NZ
    spot = (head // 32) * 4 + head % 4
    ahead = (plane - z + NZ) % NZ
    up = ((ahead >= 1) & (ahead <= 3)) | ((ahead == 4) & (spot < 8))
    far_up = jnp.max(jnp.where(up, ahead, 0), axis=1)
    far_down = jnp.max(jnp.where(up | (ahead == 0), 0, NZ - ahead), axis=1)
    number = jnp.arange(blocks, dtype=jnp.int32)

    def place(far):
        first = (far[None, :] > far[:, None]) | (
            (far[None, :] == far[:, None]) & (number[None, :] < number[:, None])
        )
        return jnp.sum(first.astype(jnp.int32), axis=1)

    pos_up, pos_down = place(far_up), place(far_down)
    order = jnp.stack(
        [
            jnp.sum(jnp.where(pos[None, :] == number[:, None], number[None, :], 0), axis=1)
            for pos in (pos_up, pos_down)
        ]
    )
    pos = jnp.where(ahead == 0, number[:, None], jnp.where(up, pos_up[:, None], pos_down[:, None]))
    entries = blocks * top
    flat = head.reshape(entries)
    nth = jnp.arange(entries, dtype=jnp.int32)
    rank = jnp.sum(
        ((flat[None, :] == flat[:, None]) & (nth[None, :] < nth[:, None])).astype(jnp.int32), axis=1
    )
    lane = (plane * 128 + 2 * spot).reshape(entries) + rank
    picker = (lane[:, None] == jnp.arange(NZ * 128, dtype=jnp.int32)[None, :]).astype(jnp.bfloat16)
    facts = jnp.concatenate(
        [
            (labels.reshape(entries, rows) + 1).astype(jnp.bfloat16),
            jnp.broadcast_to(pos.reshape(entries, 1), (entries, 8)).astype(jnp.bfloat16),
        ],
        axis=1,
    )
    table = lax.dot_general(
        facts, picker, (((0,), (0,)), ((), ())), preferred_element_type=jnp.float32
    ).astype(jnp.int32)
    return order, table


def dispatch_kernel(
    order_ref, table_ref, emb_ref, got_ref, marks_ref,
    send_up, send_down, up_1, up_2, up_3, up_4, down_1, down_2, down_3, down_4, picked, facts, places,
    ring_send, ring_recv, fact_send, fact_recv, place_sem, own_sem,
    mark_send, mark_recv, plane_send, plane_recv,
):
    dp, x, core = lax.axis_index("dp"), lax.axis_index("head"), lax.axis_index("rep")
    y, z = dp // NZ, lax.rem(dp, NZ)
    me = y * 4 + x

    def at_plane(z_to):
        return (y * NZ + z_to, x, core)

    def in_plane(j):
        p = lax.rem(me + j, 16)
        return p, ((p // 4) * NZ + z, lax.rem(p, 4), core)

    barrier = pltpu.get_barrier_semaphore()
    for d in range(1, NZ):
        pl.semaphore_signal(
            barrier, inc=1, device_id=at_plane(lax.rem(z + d, NZ)), device_id_type=MESH
        )

    def greet(j, _):
        _, device = in_plane(j)
        pl.semaphore_signal(barrier, inc=1, device_id=device, device_id_type=MESH)
        return 0

    lax.fori_loop(1, 16, greet, 0)

    def arrange(i, _):
        send_up[i] = emb_ref[order_ref[0, i]]
        send_down[i] = emb_ref[order_ref[1, i]]
        return 0

    lax.fori_loop(0, 64, arrange, 0)
    own_facts = pltpu.make_async_copy(
        table_ref.at[:, pl.ds(pl.multiple_of(z * 128, 128), 128)], facts.at[0], own_sem
    )
    own_facts.start()
    own_facts.wait()
    pl.semaphore_wait(barrier, 22)

    fact_copies = []
    for d in range(1, NZ):
        z_to = lax.rem(z + d, NZ)
        copy = pltpu.make_async_remote_copy(
            src_ref=table_ref.at[:, pl.ds(pl.multiple_of(z_to * 128, 128), 128)],
            dst_ref=facts.at[STEP_OF[d]],
            send_sem=fact_send.at[d],
            recv_sem=fact_recv.at[STEP_OF[d]],
            device_id=at_plane(z_to),
            device_id_type=MESH,
        )
        copy.start()
        fact_copies.append(copy)

    rings = (
        (send_up, up_1, up_2, up_3, up_4),
        (send_down, down_1, down_2, down_3, down_4),
    )
    targets = (at_plane(lax.rem(z + 1, NZ)), at_plane(lax.rem(z + NZ - 1, NZ)))
    ring_copies = {}

    def hop(way, number, piece):
        low, high = CUTS[piece]
        copy = pltpu.make_async_remote_copy(
            src_ref=rings[way][number - 1].at[pl.ds(low, high - low)],
            dst_ref=rings[way][number].at[pl.ds(low, high - low)],
            send_sem=ring_send.at[way, number - 1, piece],
            recv_sem=ring_recv.at[way, number - 1, piece],
            device_id=targets[way],
            device_id_type=MESH,
        )
        copy.start()
        ring_copies[way, number, piece] = copy

    for piece in range(3):
        for way in range(2):
            hop(way, 1, piece)

    def load_places(step):
        copy = pltpu.make_async_copy(
            facts.at[step, pl.ds(8, 8)], places.at[step], place_sem.at[step]
        )
        copy.start()
        copy.wait()

    def pick(step, source, low, high):
        def one(q, _):
            picked[step, q] = source[places[step, 0, q]]
            return 0

        lax.fori_loop(low, high, one, 0)

    def spread(step):
        own = pltpu.make_async_copy(
            picked.at[step, pl.ds(2 * me, 2)], got_ref.at[step, me], own_sem
        )
        own.start()

        def send(j, _):
            p, device = in_plane(j)
            pltpu.make_async_remote_copy(
                src_ref=picked.at[step, pl.ds(2 * p, 2)],
                dst_ref=got_ref.at[step, me],
                send_sem=plane_send.at[step],
                recv_sem=plane_recv.at[step],
                device_id=device,
                device_id_type=MESH,
            ).start()
            return 0

        lax.fori_loop(1, 16, send, 0)
        own.wait()

    load_places(0)
    pick(0, emb_ref, 0, 32)
    spread(0)

    for copy in fact_copies:
        copy.wait()
    for step in range(1, NZ):
        load_places(step)

    own_marks = pltpu.make_async_copy(facts.at[:, pl.ds(0, 8)], marks_ref.at[me], own_sem)
    own_marks.start()

    def send_marks(j, _):
        _, device = in_plane(j)
        pltpu.make_async_remote_copy(
            src_ref=facts.at[:, pl.ds(0, 8)],
            dst_ref=marks_ref.at[me],
            send_sem=mark_send,
            recv_sem=mark_recv,
            device_id=device,
            device_id_type=MESH,
        ).start()
        return 0

    lax.fori_loop(1, 16, send_marks, 0)
    own_marks.wait()

    for number in range(1, 5):
        for piece in range(CUTS_AT[number]):
            for way in range(2):
                ring_copies[way, number, piece].wait_recv()
                if number < 4 and piece < CUTS_AT[number + 1]:
                    hop(way, number + 1, piece)
        if number < 4:
            for way in range(2):
                pick(2 * number - 1 + way, rings[way][number], 0, 32)
                spread(2 * number - 1 + way)
        else:
            pick(7, up_4, 0, 16)
            pick(7, down_4, 16, 32)
            spread(7)

    for copy in ring_copies.values():
        copy.wait_send()
    whole = marks_ref.at[pl.ds(0, 15)]
    pltpu.make_async_copy(whole, whole, mark_send).wait()
    pltpu.make_async_copy(whole, whole, mark_recv).wait()
    for step in range(NZ):
        whole = got_ref.at[step, pl.ds(0, 15)]
        pltpu.make_async_copy(whole, whole, plane_send.at[step]).wait()
        pltpu.make_async_copy(whole, whole, plane_recv.at[step]).wait()


def dispatch(order, table, embeddings):
    feature = embeddings.shape[2]
    bf16, i32 = jnp.bfloat16, jnp.int32
    dma = pltpu.SemaphoreType.DMA
    return pl.pallas_call(
        dispatch_kernel,
        out_shape=(
            jax.ShapeDtypeStruct((NZ, 16, 2, 8, feature), bf16),
            jax.ShapeDtypeStruct((16, NZ, 8, 128), i32),
        ),
        in_specs=[
            pl.BlockSpec(memory_space=pltpu.SMEM),
            pl.BlockSpec(memory_space=pltpu.VMEM),
            pl.BlockSpec(memory_space=pltpu.VMEM),
        ],
        out_specs=(
            pl.BlockSpec(memory_space=pltpu.VMEM),
            pl.BlockSpec(memory_space=pltpu.VMEM),
        ),
        scratch_shapes=[
            pltpu.VMEM((64, 8, feature), bf16),
            pltpu.VMEM((64, 8, feature), bf16),
            *[pltpu.VMEM((size, 8, feature), bf16) for size in HOP_SIZE * 2],
            pltpu.VMEM((NZ, 32, 8, feature), bf16),
            pltpu.VMEM((NZ, 16, 128), i32),
            pltpu.SMEM((NZ, 8, 128), i32),
            dma((2, 4, 3)),
            dma((2, 4, 3)),
            dma((NZ,)),
            dma((NZ,)),
            dma((NZ,)),
            dma,
            dma,
            dma,
            dma((NZ,)),
            dma((NZ,)),
        ],
        compiler_params=pltpu.CompilerParams(
            collective_id=0, has_side_effects=True, vmem_limit_bytes=60 << 20
        ),
        name="dispatch",
    )(order, table, embeddings)


def per_device(
    embeddings, coverage, labels, w_in, bias_in, w_out, first_w, second_w, first_vec, second_vec
):
    feature = embeddings.shape[2]
    z = lax.rem(lax.axis_index("dp"), NZ)
    me = (lax.axis_index("dp") // NZ) * 4 + lax.axis_index("head")
    order, table = plan(coverage, labels, z)
    got, marks = dispatch(order, table, embeddings)
    row_data = got.reshape(-1, feature)
    own = lax.dynamic_slice_in_dim(marks, 2 * me, 2, 3)
    marks_all = jnp.transpose(own, (1, 0, 3, 2)).reshape(-1).astype(jnp.float32)
    usable = marks_all > 0.5
    target = marks_all - 1.0
    out_weight = w_out[0].astype(jnp.float32)
    pre_act = (
        jnp.dot(row_data, w_in[0], preferred_element_type=jnp.float32)
        + bias_in[0].astype(jnp.float32)[None, :]
    )
    sig_pre = jax.nn.sigmoid(pre_act)
    hidden = pre_act * sig_pre
    logits = jnp.sum(hidden * out_weight[None, :], axis=1)
    residual = jnp.where(usable, jax.nn.sigmoid(logits) - target, jnp.zeros_like(logits))
    grad_pre = residual[:, None] * out_weight[None, :] * sig_pre * (1.0 + pre_act * (1.0 - sig_pre))
    grad_low = grad_pre.astype(jnp.bfloat16)
    vec_part = jnp.stack([jnp.sum(grad_pre, axis=0), jnp.sum(residual[:, None] * hidden, axis=0)])
    half_rows = feature // lax.axis_size("rep")
    first_row = lax.axis_index("rep") * half_rows
    full_part = lax.dot_general(
        row_data, grad_low, (((0,), (0,)), ((), ())), preferred_element_type=jnp.float32
    )
    whole_w, grad_vec = lax.psum((full_part, vec_part), "rep")
    grad_w = lax.dynamic_slice_in_dim(whole_w, first_row, half_rows, 0)
    new_first_w = beta_one * first_w[0] + (1.0 - beta_one) * grad_w
    new_second_w = beta_two * second_w[0] + (1.0 - beta_two) * grad_w * grad_w
    old_rows = lax.dynamic_slice_in_dim(w_in[0], first_row, half_rows, 0).astype(jnp.float32)
    new_half = (old_rows - learn_rate * new_first_w / (jnp.sqrt(new_second_w) + epsilon)).astype(
        jnp.bfloat16
    )
    new_w_in = lax.all_gather(new_half, "rep", axis=0, tiled=True)
    vector = jnp.stack([bias_in[0], w_out[0]]).astype(jnp.float32)
    new_first_vec = beta_one * first_vec[0] + (1.0 - beta_one) * grad_vec
    new_second_vec = beta_two * second_vec[0] + (1.0 - beta_two) * grad_vec * grad_vec
    new_vec = (vector - learn_rate * new_first_vec / (jnp.sqrt(new_second_vec) + epsilon)).astype(
        jnp.bfloat16
    )
    return (
        new_w_in[None],
        new_vec[None],
        new_first_w[None],
        new_second_w[None],
        new_first_vec[None],
        new_second_vec[None],
    )


def solution(mesh):
    owners = ("dp", "head")
    moments = P(owners, "rep", None)
    vectors = P(owners, None, None)
    everyone = ("dp", "head", "rep")
    placed = (
        P(everyone, None, None),
        P(everyone, None),
        P(everyone, None, None),
        vectors,
        P(owners, None),
        P(owners, None),
        moments,
        moments,
        vectors,
        vectors,
    )
    return jax.shard_map(
        per_device,
        mesh=mesh,
        in_specs=placed,
        out_specs=(vectors, vectors, moments, moments, vectors, vectors),
        check_vma=False,
    )
```

```python
import jax
import jax.numpy as jnp
from jax import lax
from jax.experimental import pallas as pl
from jax.experimental.pallas import tpu as pltpu
from jax.sharding import PartitionSpec as P

beta_one = 0.9
beta_two = 0.999
learn_rate = 0.001
epsilon = 1e-08

MESH = pl.DeviceIdType.MESH
NZ = 8
STEP_OF = (0, 1, 3, 5, 7, 6, 4, 2)
CUTS = ((0, 16), (16, 48), (48, 64))
CUTS_AT = {1: 3, 2: 3, 3: 2, 4: 1}
HOP_SIZE = (64, 64, 48, 16)


def plan(coverage, labels, z):
    blocks, top = coverage.shape
    rows = labels.shape[2]
    head = coverage
    plane = (head // 4) % NZ
    spot = (head // 32) * 4 + head % 4
    ahead = (plane - z + NZ) % NZ
    up = ((ahead >= 1) & (ahead <= 3)) | ((ahead == 4) & (spot < 8))
    far_up = jnp.max(jnp.where(up, ahead, 0), axis=1)
    far_down = jnp.max(jnp.where(up | (ahead == 0), 0, NZ - ahead), axis=1)
    number = jnp.arange(blocks, dtype=jnp.int32)

    def place(far):
        first = (far[None, :] > far[:, None]) | (
            (far[None, :] == far[:, None]) & (number[None, :] < number[:, None])
        )
        return jnp.sum(first.astype(jnp.int32), axis=1)

    pos_up, pos_down = place(far_up), place(far_down)
    order = jnp.stack(
        [
            jnp.sum(jnp.where(pos[None, :] == number[:, None], number[None, :], 0), axis=1)
            for pos in (pos_up, pos_down)
        ]
    )
    pos = jnp.where(ahead == 0, number[:, None], jnp.where(up, pos_up[:, None], pos_down[:, None]))
    entries = blocks * top
    flat = head.reshape(entries)
    nth = jnp.arange(entries, dtype=jnp.int32)
    rank = jnp.sum(
        ((flat[None, :] == flat[:, None]) & (nth[None, :] < nth[:, None])).astype(jnp.int32), axis=1
    )
    lane = (plane * 128 + spot).reshape(entries) + 16 * rank
    picker = (lane[:, None] == jnp.arange(NZ * 128, dtype=jnp.int32)[None, :]).astype(jnp.bfloat16)
    facts = jnp.concatenate(
        [
            (labels.reshape(entries, rows) + 1).astype(jnp.bfloat16),
            jnp.broadcast_to(pos.reshape(entries, 1), (entries, 8)).astype(jnp.bfloat16),
        ],
        axis=1,
    )
    table = lax.dot_general(
        facts, picker, (((0,), (0,)), ((), ())), preferred_element_type=jnp.float32
    ).astype(jnp.int32)
    return order, table


def step_kernel(
    order_ref, table_ref, emb_ref, bias_ref, out_w_ref, first_vec_ref, second_vec_ref,
    w_hbm, first_hbm, second_hbm,
    new_vec_ref, new_first_vec_ref, new_second_vec_ref, new_w_hbm, new_first_hbm, new_second_hbm,
    send_up, send_down, up_1, up_2, up_3, up_4, down_1, down_2, down_3, down_4,
    picked, got, facts, marks, w_ref, first_ref, second_ref, new_first, new_second, new_w,
    pre_ref, low_ref, turned, total, other, vec_total, vec_other, mark_col, places,
    ring_send, ring_recv, fact_send, fact_recv, place_sem, own_sem,
    mark_send, mark_recv, plane_send, plane_recv, load_sem, swap_send, swap_recv, out_sem,
):
    dp, x, core = lax.axis_index("dp"), lax.axis_index("head"), lax.axis_index("rep")
    y, z = dp // NZ, lax.rem(dp, NZ)
    me = y * 4 + x
    partner = (dp, x, 1 - core)
    feature, hid = w_ref.shape
    half = feature // 2
    piece_rows = half // 2
    f32 = jnp.float32

    def at_plane(z_to):
        return (y * NZ + z_to, x, core)

    def in_plane(j):
        p = lax.rem(me + j, 16)
        return p, ((p // 4) * NZ + z, lax.rem(p, 4), core)

    barrier = pltpu.get_barrier_semaphore()
    for d in range(1, NZ):
        pl.semaphore_signal(
            barrier, inc=1, device_id=at_plane(lax.rem(z + d, NZ)), device_id_type=MESH
        )

    def greet(j, _):
        _, device = in_plane(j)
        pl.semaphore_signal(barrier, inc=1, device_id=device, device_id_type=MESH)
        return 0

    lax.fori_loop(1, 16, greet, 0)
    pl.semaphore_signal(barrier, inc=1, device_id=partner, device_id_type=MESH)

    def arrange(i, _):
        send_up[i] = emb_ref[order_ref[0, i]]
        send_down[i] = emb_ref[order_ref[1, i]]
        return 0

    lax.fori_loop(0, 64, arrange, 0)
    own_facts = pltpu.make_async_copy(
        table_ref.at[:, pl.ds(pl.multiple_of(z * 128, 128), 128)], facts.at[0], own_sem
    )
    own_facts.start()
    own_facts.wait()
    pl.semaphore_wait(barrier, 23)

    rings = (
        (send_up, up_1, up_2, up_3, up_4),
        (send_down, down_1, down_2, down_3, down_4),
    )
    targets = (at_plane(lax.rem(z + 1, NZ)), at_plane(lax.rem(z + NZ - 1, NZ)))
    ring_copies = {}

    def hop(way, number, piece):
        low, high = CUTS[piece]
        copy = pltpu.make_async_remote_copy(
            src_ref=rings[way][number - 1].at[pl.ds(low, high - low)],
            dst_ref=rings[way][number].at[pl.ds(low, high - low)],
            send_sem=ring_send.at[way, number - 1, piece],
            recv_sem=ring_recv.at[way, number - 1, piece],
            device_id=targets[way],
            device_id_type=MESH,
        )
        copy.start()
        ring_copies[way, number, piece] = copy

    fact_copies = []
    for d in range(1, NZ):
        z_to = lax.rem(z + d, NZ)
        copy = pltpu.make_async_remote_copy(
            src_ref=table_ref.at[:, pl.ds(pl.multiple_of(z_to * 128, 128), 128)],
            dst_ref=facts.at[STEP_OF[d]],
            send_sem=fact_send.at[d],
            recv_sem=fact_recv.at[STEP_OF[d]],
            device_id=at_plane(z_to),
            device_id_type=MESH,
        )
        copy.start()
        fact_copies.append(copy)

    for piece in range(3):
        for way in range(2):
            hop(way, 1, piece)

    loads = [
        pltpu.make_async_copy(src, dst, load_sem.at[i])
        for i, (src, dst) in enumerate(
            ((w_hbm, w_ref), (first_hbm, first_ref), (second_hbm, second_ref))
        )
    ]
    for load in loads:
        load.start()

    def load_places(step):
        copy = pltpu.make_async_copy(
            facts.at[step, pl.ds(8, 8)], places.at[step], place_sem.at[step]
        )
        copy.start()
        copy.wait()

    def pick(step, way, source):
        low, high = (0, 16) if way is None else ((0, 8), (8, 16))[way]

        def one(p, _):
            picked[step, 0, p] = source[places[step, 0, p]]
            picked[step, 1, p] = source[places[step, 0, 16 + p]]
            return 0

        lax.fori_loop(low, high, one, 0)

    def spread(step):
        own = pltpu.make_async_copy(picked.at[step, :, me], got.at[step, :, me], own_sem)
        own.start()

        def send(j, _):
            p, device = in_plane(j)
            pltpu.make_async_remote_copy(
                src_ref=picked.at[step, :, p],
                dst_ref=got.at[step, :, me],
                send_sem=plane_send.at[step],
                recv_sem=plane_recv.at[step],
                device_id=device,
                device_id_type=MESH,
            ).start()
            return 0

        lax.fori_loop(1, 16, send, 0)
        own.wait()

    def received(step):
        whole = got.at[step, :, pl.ds(0, 15)]
        pltpu.make_async_copy(whole, whole, plane_recv.at[step]).wait()

    def forward(step):
        rows = got[step].reshape(256, feature)
        pre_ref[...] = jnp.dot(rows, w_ref[...], preferred_element_type=f32) + bias_ref[...].astype(f32)
        turned[...] = rows.T
        mine = marks[:, step].astype(f32).reshape(128, 128)
        lanes = lax.broadcasted_iota(jnp.int32, (128, 128), 1)
        for k in range(2):
            picked_marks = jnp.where(lanes == me + 16 * k, mine, 0.0)
            mark_col[pl.ds(128 * k, 128)] = jnp.sum(picked_marks, axis=1, keepdims=True)

        out_w = out_w_ref[...].astype(f32)

        def group(i, _):
            at = pl.ds(pl.multiple_of(i * 16, 16), 16)
            pre = pre_ref[at]
            mark = mark_col[at]
            sig = 1.0 / (1.0 + jnp.exp(-pre))
            hidden = pre * sig
            logits = jnp.sum(hidden * out_w, axis=1, keepdims=True)
            guess = 1.0 / (1.0 + jnp.exp(-logits))
            residual = jnp.where(mark > 0.5, guess - (mark - 1.0), 0.0)
            grad_pre = residual * out_w * sig * (1.0 + pre * (1.0 - sig))
            low_ref[at] = grad_pre.astype(jnp.bfloat16)
            vec_total[0] += grad_pre[0:8] + grad_pre[8:16]
            swing = residual * hidden
            vec_total[1] += swing[0:8] + swing[8:16]
            return 0

        lax.fori_loop(0, 16, group, 0)

    def gradient(low):
        at = pl.ds(pl.multiple_of(low, 16), piece_rows)
        total[at] += jnp.dot(turned[at], low_ref[...], preferred_element_type=f32)

    def learn(step, _):
        received(step)
        forward(step)
        lax.fori_loop(0, 4, lambda i, _: (gradient(i * piece_rows), 0)[1], 0)
        return 0

    load_places(0)
    pick(0, None, emb_ref)
    spread(0)

    total[...] = jnp.zeros_like(total)
    vec_total[...] = jnp.zeros_like(vec_total)

    for copy in fact_copies:
        copy.wait()
    for step in range(1, NZ):
        load_places(step)

    own_marks = pltpu.make_async_copy(facts.at[:, pl.ds(0, 8)], marks.at[me], own_sem)
    own_marks.start()

    def send_marks(j, _):
        _, device = in_plane(j)
        pltpu.make_async_remote_copy(
            src_ref=facts.at[:, pl.ds(0, 8)],
            dst_ref=marks.at[me],
            send_sem=mark_send,
            recv_sem=mark_recv,
            device_id=device,
            device_id_type=MESH,
        ).start()
        return 0

    lax.fori_loop(1, 16, send_marks, 0)
    own_marks.wait()
    for load in loads:
        load.wait()

    for number in range(1, 5):
        for piece in range(CUTS_AT[number]):
            for way in range(2):
                ring_copies[way, number, piece].wait_recv()
                if number < 4 and piece < CUTS_AT[number + 1]:
                    hop(way, number + 1, piece)
        if number < 4:
            for way in range(2):
                pick(2 * number - 1 + way, None, rings[way][number])
                spread(2 * number - 1 + way)
        else:
            pick(7, 0, up_4)
            pick(7, 1, down_4)
            spread(7)
        if number == 1:
            whole = marks.at[pl.ds(0, 15)]
            pltpu.make_async_copy(whole, whole, mark_recv).wait()
            lax.fori_loop(0, 1, learn, 0)
        elif number < 4:
            lax.fori_loop(2 * number - 3, 2 * number - 1, learn, 0)

    lax.fori_loop(5, 7, learn, 0)
    received(7)
    forward(7)

    ours = core * half
    theirs = half - ours

    def swap(i):
        copy = pltpu.make_async_remote_copy(
            src_ref=total.at[pl.ds(pl.multiple_of(theirs + i * piece_rows, 16), piece_rows)],
            dst_ref=other.at[pl.ds(i * piece_rows, piece_rows)],
            send_sem=swap_send.at[i],
            recv_sem=swap_recv.at[i],
            device_id=partner,
            device_id_type=MESH,
        )
        copy.start()
        return copy

    gradient(theirs)
    gradient(theirs + piece_rows)
    swaps = [swap(0)]
    vec_swap = pltpu.make_async_remote_copy(
        src_ref=vec_total,
        dst_ref=vec_other,
        send_sem=swap_send.at[2],
        recv_sem=swap_recv.at[2],
        device_id=partner,
        device_id_type=MESH,
    )
    vec_swap.start()
    gradient(ours)
    swaps.append(swap(1))
    gradient(ours + piece_rows)

    vec_swap.wait_recv()
    vec_sum = vec_total[...] + vec_other[...]
    grad_vec = jnp.sum(vec_sum, axis=1)
    new_first_vec = beta_one * first_vec_ref[...] + (1.0 - beta_one) * grad_vec
    new_second_vec = beta_two * second_vec_ref[...] + (1.0 - beta_two) * grad_vec * grad_vec
    vector = jnp.concatenate([bias_ref[...].astype(f32), out_w_ref[...].astype(f32)], axis=0)
    new_first_vec_ref[...] = new_first_vec
    new_second_vec_ref[...] = new_second_vec
    new_vec_ref[...] = (
        vector - learn_rate * new_first_vec / (jnp.sqrt(new_second_vec) + epsilon)
    ).astype(jnp.bfloat16)

    copies = []
    for i in range(2):
        swaps[i].wait_recv()

        def adam(r, _):
            here = pl.multiple_of(i * piece_rows + r * 16, 16)
            at = pl.ds(here, 16)
            there = pl.ds(pl.multiple_of(ours + here, 16), 16)
            grad = total[there] + other[at]
            first = beta_one * first_ref[at] + (1.0 - beta_one) * grad
            second = beta_two * second_ref[at] + (1.0 - beta_two) * grad * grad
            new_first[at] = first
            new_second[at] = second
            new_w[at] = (
                w_ref[there].astype(f32) - learn_rate * first / (jnp.sqrt(second) + epsilon)
            ).astype(jnp.bfloat16)
            return 0

        lax.fori_loop(0, piece_rows // 16, adam, 0)
        at = pl.ds(i * piece_rows, piece_rows)
        there = pl.ds(pl.multiple_of(ours + i * piece_rows, 16), piece_rows)
        for k, (src, dst) in enumerate(((new_first, new_first_hbm), (new_second, new_second_hbm))):
            copy = pltpu.make_async_copy(src.at[at], dst.at[at], out_sem.at[k, i])
            copy.start()
            copies.append(copy)
        copy = pltpu.make_async_remote_copy(
            src_ref=new_w.at[at],
            dst_ref=new_w_hbm.at[there],
            send_sem=swap_send.at[3 + i],
            recv_sem=swap_recv.at[3 + i],
            device_id=partner,
            device_id_type=MESH,
        )
        copy.start()
        copies.append(copy)
        copy = pltpu.make_async_copy(new_w.at[at], new_w_hbm.at[there], out_sem.at[2, i])
        copy.start()
        copies.append(copy)

    vec_swap.wait_send()
    for copy in swaps:
        copy.wait_send()
    for copy in ring_copies.values():
        copy.wait_send()
    whole = marks.at[pl.ds(0, 15)]
    pltpu.make_async_copy(whole, whole, mark_send).wait()
    for step in range(NZ):
        whole = got.at[step, :, pl.ds(0, 15)]
        pltpu.make_async_copy(whole, whole, plane_send.at[step]).wait()
    for copy in copies:
        copy.wait()


def per_device(
    embeddings, coverage, labels, w_in, bias_in, w_out, first_w, second_w, first_vec, second_vec
):
    feature = embeddings.shape[2]
    hid = w_in.shape[2]
    half = feature // 2
    z = lax.rem(lax.axis_index("dp"), NZ)
    order, table = plan(coverage, labels, z)
    bf16, i32, f32 = jnp.bfloat16, jnp.int32, jnp.float32
    dma, vmem = pltpu.SemaphoreType.DMA, pltpu.VMEM
    smem_in = pl.BlockSpec(memory_space=pltpu.SMEM)
    vmem_in = pl.BlockSpec(memory_space=vmem)
    any_in = pl.BlockSpec(memory_space=pl.ANY)
    new_vec, new_first_vec, new_second_vec, new_w, new_first, new_second = pl.pallas_call(
        step_kernel,
        out_shape=(
            jax.ShapeDtypeStruct((2, hid), bf16),
            jax.ShapeDtypeStruct((2, hid), f32),
            jax.ShapeDtypeStruct((2, hid), f32),
            jax.ShapeDtypeStruct((feature, hid), bf16),
            jax.ShapeDtypeStruct((half, hid), f32),
            jax.ShapeDtypeStruct((half, hid), f32),
        ),
        in_specs=[smem_in, *[vmem_in] * 6, *[any_in] * 3],
        out_specs=(*[vmem_in] * 3, *[any_in] * 3),
        scratch_shapes=[
            vmem((64, 8, feature), bf16),
            vmem((64, 8, feature), bf16),
            *[vmem((size, 8, feature), bf16) for size in HOP_SIZE * 2],
            vmem((NZ, 2, 16, 8, feature), bf16),
            vmem((NZ, 2, 16, 8, feature), bf16),
            vmem((NZ, 16, 128), i32),
            vmem((16, NZ, 8, 128), i32),
            vmem((feature, hid), bf16),
            vmem((half, hid), f32),
            vmem((half, hid), f32),
            vmem((half, hid), f32),
            vmem((half, hid), f32),
            vmem((half, hid), bf16),
            vmem((256, hid), f32),
            vmem((256, hid), bf16),
            vmem((feature, 256), bf16),
            vmem((feature, hid), f32),
            vmem((half, hid), f32),
            vmem((2, 8, hid), f32),
            vmem((2, 8, hid), f32),
            vmem((256, 1), f32),
            pltpu.SMEM((NZ, 8, 128), i32),
            dma((2, 4, 3)),
            dma((2, 4, 3)),
            dma((NZ,)),
            dma((NZ,)),
            dma((NZ,)),
            dma,
            dma,
            dma,
            dma((NZ,)),
            dma((NZ,)),
            dma((3,)),
            dma((5,)),
            dma((5,)),
            dma((3, 2)),
        ],
        compiler_params=pltpu.CompilerParams(
            collective_id=0, has_side_effects=True, vmem_limit_bytes=60 << 20
        ),
        name="adam_step",
    )(
        order, table, embeddings, bias_in, w_out, first_vec[0], second_vec[0],
        w_in[0], first_w[0], second_w[0],
    )
    return (
        new_w[None],
        new_vec[None],
        new_first[None],
        new_second[None],
        new_first_vec[None],
        new_second_vec[None],
    )


def solution(mesh):
    owners = ("dp", "head")
    moments = P(owners, "rep", None)
    vectors = P(owners, None, None)
    everyone = ("dp", "head", "rep")
    placed = (
        P(everyone, None, None),
        P(everyone, None),
        P(everyone, None, None),
        vectors,
        P(owners, None),
        P(owners, None),
        moments,
        moments,
        vectors,
        vectors,
    )
    return jax.shard_map(
        per_device,
        mesh=mesh,
        in_specs=placed,
        out_specs=(vectors, vectors, moments, moments, vectors, vectors),
        check_vma=False,
    )
```

```python
import jax
import jax.numpy as jnp
from jax import lax
from jax.experimental import pallas as pl
from jax.experimental.pallas import tpu as pltpu
from jax.sharding import PartitionSpec as P

beta_one = 0.9
beta_two = 0.999
learn_rate = 0.001
epsilon = 1e-08

MESH = pl.DeviceIdType.MESH
NZ = 8
STEP_OF = (0, 1, 3, 5, 7, 6, 4, 2)
PIECES = {
    1: ((0, 24), (24, 48), (48, 64)),
    2: ((0, 24), (24, 48), (48, 64)),
    3: ((0, 24), (24, 32), (32, 40), (40, 48)),
    4: ((0, 16),),
}


def plan_kernel(cover_ref, labels_ref, order_ref, table_ref):
    z = lax.rem(lax.axis_index("dp"), NZ)
    f32, i32, bf16 = jnp.float32, jnp.int32, jnp.bfloat16
    blocks = 64
    square = (blocks, blocks)
    down_axis = lax.broadcasted_iota(i32, square, 0)
    along = lax.broadcasted_iota(i32, square, 1)
    number = lax.broadcasted_iota(i32, (1, blocks), 1)

    def upright(row):
        spread = jnp.where(down_axis == along, jnp.broadcast_to(row, square), 0)
        return jnp.sum(spread.astype(f32), axis=1, keepdims=True).astype(i32)

    def count(flags):
        return jnp.sum(jnp.where(flags, 1.0, 0.0), axis=0, keepdims=True).astype(i32)

    heads = [cover_ref[t : t + 1] for t in range(2)]
    ahead, spot, up, far_up, far_down = [], [], [], None, None
    for head in heads:
        plane = (head >> 2) & 7
        x, y = head & 3, head >> 5
        kind = (x + y) & 3
        gap = (plane - z + NZ) & 7
        is_up = ((gap >= 1) & (gap <= 3)) | ((gap == 4) & (kind < 2))
        is_down = (gap >= 5) | ((gap == 4) & (kind >= 2))
        rank_up = jnp.where(gap == 4, 9, jnp.where(gap == 3, 8 - kind, 0))
        rank_down = jnp.where(gap == 4, 9, jnp.where(gap == 5, 8 - kind, 0))
        rank_up = jnp.where(is_up, rank_up, 0)
        rank_down = jnp.where(is_down, rank_down, 0)
        far_up = rank_up if far_up is None else jnp.maximum(far_up, rank_up)
        far_down = rank_down if far_down is None else jnp.maximum(far_down, rank_down)
        ahead.append(gap)
        spot.append(4 * kind + x)
        up.append(is_up)

    places, orders = [], []
    for far in (far_up, far_down):
        tall = upright(far)
        pos = count((tall > far) | ((tall == far) & (down_axis < along)))
        places.append(pos)
        order = jnp.sum(
            jnp.where(upright(pos) == along, down_axis, 0).astype(f32), axis=0, keepdims=True
        )
        orders.append(order.astype(i32))
    order_ref[0:1] = orders[0]
    order_ref[1:2] = orders[1]

    tall_heads = [upright(head) for head in heads]
    earlier = down_axis < along
    ranks = [
        count((tall_heads[0] == heads[0]) & earlier),
        count(tall_heads[0] == heads[1]) + count((tall_heads[1] == heads[1]) & earlier),
    ]
    row = lax.broadcasted_iota(i32, (8, blocks), 0)
    lanes = lax.broadcasted_iota(i32, (blocks, NZ * 128), 1)
    table = None
    for t in range(2):
        plane, gap = (heads[t] >> 2) & 7, ahead[t]
        step = jnp.where(gap < 4, jnp.maximum(2 * gap - 1, 0), jnp.where(gap == 4, 7, 2 * (NZ - gap)))
        lane = plane * 128 + step * 16 + spot[t]
        picker = jnp.where(upright(lane) == lanes, 1.0, 0.0).astype(bf16)
        pos = jnp.where(gap == 0, number, jnp.where(up[t], places[0], places[1]))
        mark = labels_ref[t] + 1
        rank = jnp.broadcast_to(ranks[t], (8, blocks))
        tall_pos = jnp.broadcast_to(pos, (8, blocks))
        facts = jnp.concatenate(
            [
                jnp.where(rank == 0, mark, 0).astype(f32),
                jnp.where(rank == 1, mark, 0).astype(f32),
                jnp.where(rank == row, tall_pos, 0).astype(f32),
            ],
            axis=0,
        ).astype(bf16)
        part = jnp.dot(facts, picker, preferred_element_type=f32)
        table = part if table is None else table + part
    table_ref[...] = table.astype(i32)


def step_kernel(
    order_ref, table_ref, emb_ref, bias_ref, out_w_ref, first_vec_ref, second_vec_ref,
    w_hbm, first_hbm, second_hbm,
    new_vec_ref, new_first_vec_ref, new_second_vec_ref, new_w_hbm, new_first_hbm, new_second_hbm,
    send_up, send_down,
    up_1, up_2, up_3a, up_3b, up_3c, up_3d, up_4,
    down_1, down_2, down_3a, down_3b, down_3c, down_3d, down_4,
    up_3, down_3, picked, got, facts, own_marks, marks, w_ref, first_ref, second_ref, new_first, new_second, new_w,
    pre_ref, low_ref, turned, total, other, vec_total, vec_other, mark_col, places,
    ring_send, ring_recv, fact_send, fact_recv, place_sem, own_sem,
    mark_send, mark_recv, plane_send, plane_recv, load_sem, swap_send, swap_recv, out_sem,
):
    dp, x, core = lax.axis_index("dp"), lax.axis_index("head"), lax.axis_index("rep")
    y, z = dp // NZ, lax.rem(dp, NZ)
    me = 4 * lax.rem(x + y, 4) + x
    partner = (dp, x, 1 - core)
    feature, hid = w_ref.shape
    half = feature // 2
    piece_rows = half // 2
    f32 = jnp.float32

    def at_plane(z_to):
        return (y * NZ + z_to, x, core)

    def spot_device(p):
        x_to = lax.rem(p, 4)
        return (lax.rem(p // 4 - x_to + 4, 4) * NZ + z, x_to, core)

    barrier = pltpu.get_barrier_semaphore()
    for d in range(1, NZ):
        pl.semaphore_signal(
            barrier, inc=1, device_id=at_plane(lax.rem(z + d, NZ)), device_id_type=MESH
        )

    def greet(j, _):
        device = spot_device(lax.rem(me + j, 16))
        pl.semaphore_signal(barrier, inc=1, device_id=device, device_id_type=MESH)
        return 0

    lax.fori_loop(1, 16, greet, 0)
    pl.semaphore_signal(barrier, inc=1, device_id=partner, device_id_type=MESH)

    def arrange(i, _):
        send_up[i] = emb_ref[order_ref[0, i]]
        send_down[i] = emb_ref[order_ref[1, i]]
        return 0

    lax.fori_loop(0, 64, arrange, 0, unroll=4)
    own_facts = pltpu.make_async_copy(
        table_ref.at[:, pl.ds(pl.multiple_of(z * 128, 128), 128)], facts.at[0], load_sem.at[3]
    )
    own_facts.start()
    pl.semaphore_wait(barrier, 23)

    def whole(ref, number):
        return [ref.at[pl.ds(low, high - low)] for low, high in PIECES[number]]

    thirds = ((up_3a, up_3b, up_3c, up_3d), (down_3a, down_3b, down_3c, down_3d))
    arrivals = (
        {1: whole(up_1, 1), 2: whole(up_2, 2), 3: thirds[0], 4: (up_4,)},
        {1: whole(down_1, 1), 2: whole(down_2, 2), 3: thirds[1], 4: (down_4,)},
    )
    targets = (at_plane(lax.rem(z + 1, NZ)), at_plane(lax.rem(z + NZ - 1, NZ)))
    sources = ({1: send_up, 2: up_1, 3: up_2}, {1: send_down, 2: down_1, 3: down_2})
    ring_copies = {}

    def hop(way, number, piece):
        low, high = PIECES[number][piece]
        src = thirds[way][0] if number == 4 else sources[way][number]
        copy = pltpu.make_async_remote_copy(
            src_ref=src.at[pl.ds(low, high - low)],
            dst_ref=arrivals[way][number][piece],
            send_sem=ring_send.at[way, number - 1, piece],
            recv_sem=ring_recv.at[way, number - 1, piece],
            device_id=targets[way],
            device_id_type=MESH,
        )
        copy.start()
        ring_copies[way, number, piece] = copy

    fact_copies = []
    for d in range(1, NZ):
        z_to = lax.rem(z + d, NZ)
        copy = pltpu.make_async_remote_copy(
            src_ref=table_ref.at[:, pl.ds(pl.multiple_of(z_to * 128, 128), 128)],
            dst_ref=facts.at[STEP_OF[d]],
            send_sem=fact_send.at[d],
            recv_sem=fact_recv.at[STEP_OF[d]],
            device_id=at_plane(z_to),
            device_id_type=MESH,
        )
        copy.start()
        fact_copies.append(copy)

    for piece in range(3):
        for way in range(2):
            hop(way, 1, piece)

    loads = [
        pltpu.make_async_copy(src, dst, load_sem.at[i])
        for i, (src, dst) in enumerate(
            ((w_hbm, w_ref), (first_hbm, first_ref), (second_hbm, second_ref))
        )
    ]
    for load in loads:
        load.start()

    def pick(step, source, first, last):
        def one(p, _):
            for k in range(2):
                picked[step, k, p] = source[places[step, k, step * 16 + p]]
            return 0

        lax.fori_loop(4 * first, 4 * last, one, 0, unroll=4)

    def spread(step, first, last):
        def send(j, _):
            p = (j // 4) * 4 + lax.rem(x + j, 4)

            @pl.when(p != me)
            def _():
                pltpu.make_async_remote_copy(
                    src_ref=picked.at[step, :, p],
                    dst_ref=got.at[step, :, me],
                    send_sem=plane_send.at[step],
                    recv_sem=plane_recv.at[step],
                    device_id=spot_device(p),
                    device_id_type=MESH,
                ).start()

            @pl.when(p == me)
            def _():
                pltpu.make_async_copy(
                    picked.at[step, :, me], got.at[step, :, me], own_sem.at[step]
                ).start()

            return 0

        lax.fori_loop(4 * first, 4 * last, send, 0)

    def received(step):
        most = got.at[step, :, pl.ds(0, 15)]
        pltpu.make_async_copy(most, most, plane_recv.at[step]).wait()
        pltpu.make_async_copy(picked.at[step, :, me], got.at[step, :, me], own_sem.at[step]).wait()

    def forward(step):
        rows = got[step].reshape(256, feature)
        pre_ref[...] = jnp.dot(rows, w_ref[...], preferred_element_type=f32) + bias_ref[...].astype(f32)
        turned[...] = rows.T
        lanes = lax.broadcasted_iota(jnp.int32, (128, 128), 1)
        for k in range(2):
            every = marks[:, 8 * k : 8 * k + 8].astype(f32).reshape(128, 128)
            picked_marks = jnp.where(lanes == me + 16 * step, every, 0.0)
            mark_col[pl.ds(128 * k, 128)] = jnp.sum(picked_marks, axis=1, keepdims=True)

        out_w = out_w_ref[...].astype(f32)

        def group(i, _):
            at = pl.ds(pl.multiple_of(i * 16, 16), 16)
            pre = pre_ref[at]
            mark = mark_col[at]
            sig = 1.0 / (1.0 + jnp.exp(-pre))
            hidden = pre * sig
            logits = jnp.sum(hidden * out_w, axis=1, keepdims=True)
            guess = 1.0 / (1.0 + jnp.exp(-logits))
            residual = jnp.where(mark > 0.5, guess - (mark - 1.0), 0.0)
            grad_pre = residual * out_w * sig * (1.0 + pre * (1.0 - sig))
            low_ref[at] = grad_pre.astype(jnp.bfloat16)
            vec_total[0] += grad_pre[0:8] + grad_pre[8:16]
            swing = residual * hidden
            vec_total[1] += swing[0:8] + swing[8:16]
            return 0

        lax.fori_loop(0, 16, group, 0, unroll=4)

    def gradient(low, rows):
        at = pl.ds(pl.multiple_of(low, 16), rows)
        total[at] += jnp.dot(turned[at], low_ref[...], preferred_element_type=f32)

    def learn(step, _):
        received(step)
        forward(step)
        for i in range(2):
            gradient(i * half, half)
        return 0

    total[...] = jnp.zeros_like(total)
    vec_total[...] = jnp.zeros_like(vec_total)

    for copy in fact_copies:
        copy.wait()
    own_facts.wait()
    place_copies = []
    for step in range(NZ):
        copy = pltpu.make_async_copy(
            facts.at[step, pl.ds(16, 8)], places.at[step], place_sem.at[step]
        )
        copy.start()
        place_copies.append(copy)
    joined = facts[0, 0:16]
    for step in range(1, NZ):
        joined = joined + facts[step, 0:16]
    own_marks[...] = joined
    for copy in place_copies:
        copy.wait()
    pick(0, emb_ref, 0, 4)
    spread(0, 0, 4)
    marks[me] = joined

    def send_marks(j, _):
        pltpu.make_async_remote_copy(
            src_ref=own_marks,
            dst_ref=marks.at[me],
            send_sem=mark_send,
            recv_sem=mark_recv,
            device_id=spot_device(lax.rem(me + j, 16)),
            device_id_type=MESH,
        ).start()
        return 0

    lax.fori_loop(1, 16, send_marks, 0)
    for load in loads:
        load.wait()

    for piece in range(3):
        for way in range(2):
            ring_copies[way, 1, piece].wait_recv()
            hop(way, 2, piece)
    pick(1, up_1, 0, 4)
    pick(2, down_1, 0, 4)
    spread(1, 0, 4)
    spread(2, 0, 4)
    most_marks = marks.at[pl.ds(0, 15)]
    pltpu.make_async_copy(most_marks, most_marks, mark_recv).wait()
    lax.fori_loop(0, 1, learn, 0)

    for piece in range(3):
        for way in range(2):
            ring_copies[way, 2, piece].wait_recv()
            if piece == 0:
                hop(way, 3, 0)
            elif piece == 1:
                for part in (1, 2, 3):
                    hop(way, 3, part)
    pick(3, up_2, 0, 4)
    pick(4, down_2, 0, 4)
    spread(3, 0, 4)
    spread(4, 0, 4)
    lax.fori_loop(1, 3, learn, 0)

    for kind in range(4):
        low, high = PIECES[3][kind]
        for way, joint in enumerate((up_3, down_3)):
            ring_copies[way, 3, kind].wait_recv()
            if kind == 0:
                hop(way, 4, 0)
            joint[pl.ds(low, high - low)] = thirds[way][kind][...]
            pick(5 + way, joint, kind, kind + 1)
        spread(5, kind, kind + 1)
        spread(6, kind, kind + 1)
    lax.fori_loop(3, 5, learn, 0)

    for way, source in enumerate((up_4, down_4)):
        ring_copies[way, 4, 0].wait_recv()
        pick(7, source, 2 * way, 2 * way + 2)
    spread(7, 0, 4)
    lax.fori_loop(5, 7, learn, 0)
    received(7)
    forward(7)

    ours = core * half
    theirs = half - ours

    def swap(i):
        copy = pltpu.make_async_remote_copy(
            src_ref=total.at[pl.ds(pl.multiple_of(theirs + i * piece_rows, 16), piece_rows)],
            dst_ref=other.at[pl.ds(i * piece_rows, piece_rows)],
            send_sem=swap_send.at[i],
            recv_sem=swap_recv.at[i],
            device_id=partner,
            device_id_type=MESH,
        )
        copy.start()
        return copy

    gradient(theirs, half)
    swaps = [swap(0), swap(1)]
    vec_swap = pltpu.make_async_remote_copy(
        src_ref=vec_total,
        dst_ref=vec_other,
        send_sem=swap_send.at[2],
        recv_sem=swap_recv.at[2],
        device_id=partner,
        device_id_type=MESH,
    )
    vec_swap.start()
    gradient(ours, half)

    vec_swap.wait_recv()
    vec_sum = vec_total[...] + vec_other[...]
    grad_vec = jnp.sum(vec_sum, axis=1)
    new_first_vec = beta_one * first_vec_ref[...] + (1.0 - beta_one) * grad_vec
    new_second_vec = beta_two * second_vec_ref[...] + (1.0 - beta_two) * grad_vec * grad_vec
    vector = jnp.concatenate([bias_ref[...].astype(f32), out_w_ref[...].astype(f32)], axis=0)
    new_first_vec_ref[...] = new_first_vec
    new_second_vec_ref[...] = new_second_vec
    new_vec_ref[...] = (
        vector - learn_rate * new_first_vec / (jnp.sqrt(new_second_vec) + epsilon)
    ).astype(jnp.bfloat16)

    copies = []
    for i in range(2):
        swaps[i].wait_recv()

        def adam(r, _):
            here = pl.multiple_of(i * piece_rows + r * 16, 16)
            at = pl.ds(here, 16)
            there = pl.ds(pl.multiple_of(ours + here, 16), 16)
            grad = total[there] + other[at]
            first = beta_one * first_ref[at] + (1.0 - beta_one) * grad
            second = beta_two * second_ref[at] + (1.0 - beta_two) * grad * grad
            new_first[at] = first
            new_second[at] = second
            new_w[at] = (
                w_ref[there].astype(f32) - learn_rate * first / (jnp.sqrt(second) + epsilon)
            ).astype(jnp.bfloat16)
            return 0

        lax.fori_loop(0, piece_rows // 16, adam, 0, unroll=3)
        at = pl.ds(i * piece_rows, piece_rows)
        there = pl.ds(pl.multiple_of(ours + i * piece_rows, 16), piece_rows)
        for k, (src, dst) in enumerate(((new_first, new_first_hbm), (new_second, new_second_hbm))):
            copy = pltpu.make_async_copy(src.at[at], dst.at[at], out_sem.at[k, i])
            copy.start()
            copies.append(copy)
        copy = pltpu.make_async_remote_copy(
            src_ref=new_w.at[at],
            dst_ref=new_w_hbm.at[there],
            send_sem=swap_send.at[3 + i],
            recv_sem=swap_recv.at[3 + i],
            device_id=partner,
            device_id_type=MESH,
        )
        copy.start()
        copies.append(copy)
        copy = pltpu.make_async_copy(new_w.at[at], new_w_hbm.at[there], out_sem.at[2, i])
        copy.start()
        copies.append(copy)

    vec_swap.wait_send()
    for copy in swaps:
        copy.wait_send()
    for copy in ring_copies.values():
        copy.wait_send()
    pltpu.make_async_copy(most_marks, most_marks, mark_send).wait()
    for step in range(NZ):
        most = got.at[step, :, pl.ds(0, 15)]
        pltpu.make_async_copy(most, most, plane_send.at[step]).wait()
    for copy in copies:
        copy.wait()


def per_device(
    embeddings, coverage, labels, w_in, bias_in, w_out, first_w, second_w, first_vec, second_vec
):
    feature = embeddings.shape[2]
    hid = w_in.shape[2]
    half = feature // 2
    bf16, i32, f32 = jnp.bfloat16, jnp.int32, jnp.float32
    dma, vmem = pltpu.SemaphoreType.DMA, pltpu.VMEM
    smem_in = pl.BlockSpec(memory_space=pltpu.SMEM)
    vmem_in = pl.BlockSpec(memory_space=vmem)
    any_in = pl.BlockSpec(memory_space=pl.ANY)
    order, table = pl.pallas_call(
        plan_kernel,
        out_shape=(
            jax.ShapeDtypeStruct((2, 64), i32),
            jax.ShapeDtypeStruct((24, NZ * 128), i32),
        ),
        in_specs=[vmem_in] * 2,
        out_specs=(vmem_in, vmem_in),
        name="plan",
    )(coverage.T, labels.transpose(1, 2, 0))
    new_vec, new_first_vec, new_second_vec, new_w, new_first, new_second = pl.pallas_call(
        step_kernel,
        out_shape=(
            jax.ShapeDtypeStruct((2, hid), bf16),
            jax.ShapeDtypeStruct((2, hid), f32),
            jax.ShapeDtypeStruct((2, hid), f32),
            jax.ShapeDtypeStruct((feature, hid), bf16),
            jax.ShapeDtypeStruct((half, hid), f32),
            jax.ShapeDtypeStruct((half, hid), f32),
        ),
        in_specs=[smem_in, *[vmem_in] * 6, *[any_in] * 3],
        out_specs=(*[vmem_in] * 3, *[any_in] * 3),
        scratch_shapes=[
            vmem((64, 8, feature), bf16),
            vmem((64, 8, feature), bf16),
            *[vmem((size, 8, feature), bf16) for size in (64, 64, 24, 8, 8, 8, 16) * 2],
            vmem((48, 8, feature), bf16),
            vmem((48, 8, feature), bf16),
            vmem((NZ, 2, 16, 8, feature), bf16),
            vmem((NZ, 2, 16, 8, feature), bf16),
            vmem((NZ, 24, 128), i32),
            vmem((16, 128), i32),
            vmem((16, 16, 128), i32),
            vmem((feature, hid), bf16),
            vmem((half, hid), f32),
            vmem((half, hid), f32),
            vmem((half, hid), f32),
            vmem((half, hid), f32),
            vmem((half, hid), bf16),
            vmem((256, hid), f32),
            vmem((256, hid), bf16),
            vmem((feature, 256), bf16),
            vmem((feature, hid), f32),
            vmem((half, hid), f32),
            vmem((2, 8, hid), f32),
            vmem((2, 8, hid), f32),
            vmem((256, 1), f32),
            pltpu.SMEM((NZ, 8, 128), i32),
            dma((2, 4, 4)),
            dma((2, 4, 4)),
            dma((NZ,)),
            dma((NZ,)),
            dma((NZ,)),
            dma((NZ,)),
            dma,
            dma,
            dma((NZ,)),
            dma((NZ,)),
            dma((4,)),
            dma((5,)),
            dma((5,)),
            dma((3, 2)),
        ],
        compiler_params=pltpu.CompilerParams(
            collective_id=0, has_side_effects=True, vmem_limit_bytes=60 << 20
        ),
        name="adam_step",
    )(
        order, table, embeddings, bias_in, w_out, first_vec[0], second_vec[0],
        w_in[0], first_w[0], second_w[0],
    )
    return (
        new_w[None],
        new_vec[None],
        new_first[None],
        new_second[None],
        new_first_vec[None],
        new_second_vec[None],
    )


def solution(mesh):
    owners = ("dp", "head")
    moments = P(owners, "rep", None)
    vectors = P(owners, None, None)
    everyone = ("dp", "head", "rep")
    placed = (
        P(everyone, None, None),
        P(everyone, None),
        P(everyone, None, None),
        vectors,
        P(owners, None),
        P(owners, None),
        moments,
        moments,
        vectors,
        vectors,
    )
    return jax.shard_map(
        per_device,
        mesh=mesh,
        in_specs=placed,
        out_specs=(vectors, vectors, moments, moments, vectors, vectors),
        check_vma=False,
    )
```

```python
import jax
import jax.numpy as jnp
from jax import lax
from jax.experimental import pallas as pl
from jax.experimental.pallas import tpu as pltpu
from jax.sharding import PartitionSpec as P

beta_one = 0.9
beta_two = 0.999
learn_rate = 0.001
epsilon = 1e-08

MESH = pl.DeviceIdType.MESH
NZ = 8
STEP_OF = (0, 1, 3, 5, 7, 6, 4, 2)
PIECES = {
    1: ((0, 24), (24, 48), (48, 56), (56, 64)),
    2: ((0, 24), (24, 48), (48, 56), (56, 64)),
    3: ((0, 24), (24, 32), (32, 40), (40, 48)),
    4: ((0, 8), (8, 16)),
}


def plan_kernel(cover_ref, labels_ref, order_ref, marks_ref, spots_ref):
    z = lax.rem(lax.axis_index("dp"), NZ)
    f32, i32, bf16 = jnp.float32, jnp.int32, jnp.bfloat16
    blocks = 64
    square = (blocks, blocks)
    down_axis = lax.broadcasted_iota(i32, square, 0)
    along = lax.broadcasted_iota(i32, square, 1)
    number = lax.broadcasted_iota(i32, (1, blocks), 1)

    def upright(row):
        spread = jnp.where(down_axis == along, jnp.broadcast_to(row, square), 0)
        return jnp.sum(spread.astype(f32), axis=1, keepdims=True).astype(i32)

    def count(flags):
        return jnp.sum(jnp.where(flags, 1.0, 0.0), axis=0, keepdims=True).astype(i32)

    heads = [cover_ref[t : t + 1] for t in range(2)]
    ahead, spot, up, far_up, far_down = [], [], [], None, None
    for head in heads:
        plane = (head >> 2) & 7
        x, y = head & 3, head >> 5
        kind = (x + y) & 3
        gap = (plane - z + NZ) & 7
        is_up = ((gap >= 1) & (gap <= 3)) | ((gap == 4) & (kind < 2))
        is_down = (gap >= 5) | ((gap == 4) & (kind >= 2))
        near = jnp.where(kind == 0, 4, 0)
        rank_up = jnp.where(gap == 3, 8 - kind, jnp.where(gap == 2, near, 0))
        rank_down = jnp.where(gap == 5, 8 - kind, jnp.where(gap == 6, near, 0))
        rank_up = jnp.where(gap == 4, 10 - (kind & 1), rank_up)
        rank_down = jnp.where(gap == 4, 10 - (kind & 1), rank_down)
        rank_up = jnp.where(is_up, rank_up, 0)
        rank_down = jnp.where(is_down, rank_down, 0)
        far_up = rank_up if far_up is None else jnp.maximum(far_up, rank_up)
        far_down = rank_down if far_down is None else jnp.maximum(far_down, rank_down)
        ahead.append(gap)
        spot.append(4 * kind + x)
        up.append(is_up)

    places, orders = [], []
    for far in (far_up, far_down):
        tall = upright(far)
        pos = count((tall > far) | ((tall == far) & (down_axis < along)))
        places.append(pos)
        order = jnp.sum(
            jnp.where(upright(pos) == along, down_axis, 0).astype(f32), axis=0, keepdims=True
        )
        orders.append(order.astype(i32))
    order_ref[0:1] = orders[0]
    order_ref[1:2] = orders[1]

    tall_heads = [upright(head) for head in heads]
    earlier = down_axis < along
    ranks = [
        count((tall_heads[0] == heads[0]) & earlier),
        count(tall_heads[0] == heads[1]) + count((tall_heads[1] == heads[1]) & earlier),
    ]
    row = lax.broadcasted_iota(i32, (8, blocks), 0)
    lanes = lax.broadcasted_iota(i32, (blocks, NZ * 128), 1)
    table = None
    for t in range(2):
        plane, gap = (heads[t] >> 2) & 7, ahead[t]
        step = jnp.where(gap < 4, jnp.maximum(2 * gap - 1, 0), jnp.where(gap == 4, 7, 2 * (NZ - gap)))
        lane = plane * 128 + step * 16 + spot[t]
        picker = jnp.where(upright(lane) == lanes, 1.0, 0.0).astype(bf16)
        pos = jnp.where(gap == 0, number, jnp.where(up[t], places[0], places[1]))
        mark = labels_ref[t] + 1
        rank = jnp.broadcast_to(ranks[t], (8, blocks))
        tall_pos = jnp.broadcast_to(pos, (8, blocks))
        facts = jnp.concatenate(
            [
                jnp.where(rank == 0, mark, 0).astype(f32),
                jnp.where(rank == 1, mark, 0).astype(f32),
                jnp.where(rank == row, tall_pos, 0).astype(f32),
            ],
            axis=0,
        ).astype(bf16)
        part = jnp.dot(facts, picker, preferred_element_type=f32)
        table = part if table is None else table + part
    for plane in range(NZ):
        part = table[:, plane * 128 : plane * 128 + 128]
        marks_ref[plane] = part[0:16].astype(bf16)
        spots_ref[plane] = part[16:18].astype(i32)


def step_kernel(
    order_ref, plan_marks, plan_spots, emb_ref, bias_ref, out_w_ref, first_vec_ref, second_vec_ref,
    w_hbm, first_hbm, second_hbm,
    new_vec_ref, new_first_vec_ref, new_second_vec_ref, new_w, new_first, new_second,
    send_up, send_down,
    up_1, up_2a, up_2b, up_3a, up_3b, up_3c, up_3d, up_4a, up_4b,
    down_1, down_2a, down_2b, down_3a, down_3b, down_3c, down_3d, down_4a, down_4b,
    up_2, up_3, up_4, down_2, down_3, down_4,
    picked, got, facts, spots, own_marks, marks, w_ref, first_ref, second_ref,
    pre_ref, low_ref, low_other, turned, turned_other, total, other, vec_total, vec_other,
    mark_col, places,
    ring_send, ring_recv, fact_send, fact_recv, place_sem, own_sem,
    mark_send, mark_recv, plane_send, plane_recv, load_sem, swap_send, swap_recv,
):
    dp, x, core = lax.axis_index("dp"), lax.axis_index("head"), lax.axis_index("rep")
    y, z = dp // NZ, lax.rem(dp, NZ)
    me = 4 * lax.rem(x + y, 4) + x
    partner = (dp, x, 1 - core)
    feature, hid = w_ref.shape
    half = feature // 2
    piece_rows = half // 2
    f32 = jnp.float32

    def at_plane(z_to):
        return (y * NZ + z_to, x, core)

    def spot_device(p):
        x_to = lax.rem(p, 4)
        return (lax.rem(p // 4 - x_to + 4, 4) * NZ + z, x_to, core)

    barrier = pltpu.get_barrier_semaphore()
    for d in range(1, NZ):
        pl.semaphore_signal(
            barrier, inc=1, device_id=at_plane(lax.rem(z + d, NZ)), device_id_type=MESH
        )

    def greet(j, _):
        device = spot_device(lax.rem(me + j, 16))
        pl.semaphore_signal(barrier, inc=1, device_id=device, device_id_type=MESH)
        return 0

    lax.fori_loop(1, 16, greet, 0)
    pl.semaphore_signal(barrier, inc=1, device_id=partner, device_id_type=MESH)

    def arrange(i, _):
        send_up[i] = emb_ref[order_ref[0, i]]
        send_down[i] = emb_ref[order_ref[1, i]]
        return 0

    lax.fori_loop(0, 64, arrange, 0, unroll=4)
    tables = ((plan_marks, facts), (plan_spots, spots))
    own_tables = [
        pltpu.make_async_copy(table.at[z], held.at[0], load_sem.at[3 + i])
        for i, (table, held) in enumerate(tables)
    ]
    for copy in own_tables:
        copy.start()
    pl.semaphore_wait(barrier, 23)

    def parts(ref, number, last):
        return [ref.at[pl.ds(low, high - low)] for low, high in PIECES[number][:last]]

    arrivals = (
        {
            1: parts(up_1, 1, 4),
            2: [*parts(up_2a, 2, 3), up_2b],
            3: (up_3a, up_3b, up_3c, up_3d),
            4: (up_4a, up_4b),
        },
        {
            1: parts(down_1, 1, 4),
            2: [*parts(down_2a, 2, 3), down_2b],
            3: (down_3a, down_3b, down_3c, down_3d),
            4: (down_4a, down_4b),
        },
    )
    sources = (
        {1: send_up, 2: up_1, 3: up_2a, 4: up_3a},
        {1: send_down, 2: down_1, 3: down_2a, 4: down_3a},
    )
    joints = ({2: up_2, 3: up_3, 4: up_4}, {2: down_2, 3: down_3, 4: down_4})
    targets = (at_plane(lax.rem(z + 1, NZ)), at_plane(lax.rem(z + NZ - 1, NZ)))
    ring_copies = {}

    def hop(way, number, piece):
        low, high = PIECES[number][piece]
        copy = pltpu.make_async_remote_copy(
            src_ref=sources[way][number].at[pl.ds(low, high - low)],
            dst_ref=arrivals[way][number][piece],
            send_sem=ring_send.at[way, number - 1, piece],
            recv_sem=ring_recv.at[way, number - 1, piece],
            device_id=targets[way],
            device_id_type=MESH,
        )
        copy.start()
        ring_copies[way, number, piece] = copy

    def join(way, number, piece):
        low, high = PIECES[number][piece]
        joints[way][number][pl.ds(low, high - low)] = arrivals[way][number][piece][...]

    fact_copies = []
    for d in range(1, NZ):
        z_to = lax.rem(z + d, NZ)
        for i, (table, held) in enumerate(tables):
            copy = pltpu.make_async_remote_copy(
                src_ref=table.at[z_to],
                dst_ref=held.at[STEP_OF[d]],
                send_sem=fact_send.at[i, d],
                recv_sem=fact_recv.at[i, STEP_OF[d]],
                device_id=at_plane(z_to),
                device_id_type=MESH,
            )
            copy.start()
            fact_copies.append(copy)

    for piece in range(4):
        for way in range(2):
            hop(way, 1, piece)

    loads = [
        pltpu.make_async_copy(src, dst, load_sem.at[i])
        for i, (src, dst) in enumerate(
            ((w_hbm, w_ref), (first_hbm, first_ref), (second_hbm, second_ref))
        )
    ]
    for load in loads:
        load.start()

    def pick(step, source, first, last):
        def one(p, _):
            for k in range(2):
                picked[step, k, p] = source[places[step, k, step * 16 + p]]
            return 0

        lax.fori_loop(4 * first, 4 * last, one, 0, unroll=4)

    def spread(step, first, last):
        def send(j, _):
            p = (j // 4) * 4 + lax.rem(x + j, 4)

            @pl.when(p != me)
            def _():
                pltpu.make_async_remote_copy(
                    src_ref=picked.at[step, :, p],
                    dst_ref=got.at[step, :, me],
                    send_sem=plane_send.at[step],
                    recv_sem=plane_recv.at[step],
                    device_id=spot_device(p),
                    device_id_type=MESH,
                ).start()

            @pl.when(p == me)
            def _():
                pltpu.make_async_copy(
                    picked.at[step, :, me], got.at[step, :, me], own_sem.at[step]
                ).start()

            return 0

        lax.fori_loop(4 * first, 4 * last, send, 0)

    def received(step):
        most = got.at[step, :, pl.ds(0, 15)]
        pltpu.make_async_copy(most, most, plane_recv.at[step]).wait()
        pltpu.make_async_copy(picked.at[step, :, me], got.at[step, :, me], own_sem.at[step]).wait()

    def forward(step):
        rows = got[step].reshape(256, feature)
        turned[...] = rows.T
        pre_ref[...] = jnp.dot(rows, w_ref[...], preferred_element_type=f32) + bias_ref[...].astype(f32)
        lanes = lax.broadcasted_iota(jnp.int32, (128, 128), 1)
        every = marks[...].astype(f32)
        for k in range(2):
            mine = every[:, 8 * k : 8 * k + 8].reshape(128, 128)
            mine = jnp.where(lanes == me + 16 * step, mine, 0.0)
            mark_col[pl.ds(128 * k, 128)] = jnp.sum(mine, axis=1, keepdims=True)

        out_w = out_w_ref[...].astype(f32)

        def group(i, _):
            at = pl.ds(pl.multiple_of(i * 16, 16), 16)
            pre = pre_ref[at]
            mark = mark_col[at]
            sig = 1.0 / (1.0 + jnp.exp(-pre))
            hidden = pre * sig
            logits = jnp.sum(hidden * out_w, axis=1, keepdims=True)
            guess = 1.0 / (1.0 + jnp.exp(-logits))
            residual = jnp.where(mark > 0.5, guess - (mark - 1.0), 0.0)
            grad_pre = residual * out_w * sig * (1.0 + pre * (1.0 - sig))
            low_ref[at] = grad_pre.astype(jnp.bfloat16)
            vec_total[0] += grad_pre[0:8] + grad_pre[8:16]
            swing = residual * hidden
            vec_total[1] += swing[0:8] + swing[8:16]
            return 0

        lax.fori_loop(0, 16, group, 0, unroll=4)

    def learn(step, _):
        received(step)
        forward(step)
        for i in range(2):
            at = pl.ds(i * half, half)
            total[at] += jnp.dot(turned[at], low_ref[...], preferred_element_type=f32)
        return 0

    total[...] = jnp.zeros_like(total)
    vec_total[...] = jnp.zeros_like(vec_total)

    for copy in fact_copies:
        copy.wait()
    for copy in own_tables:
        copy.wait()
    place_copies = []
    for step in range(NZ):
        copy = pltpu.make_async_copy(
            spots.at[step], places.at[step], place_sem.at[step]
        )
        copy.start()
        place_copies.append(copy)
    joined = facts[0]
    for step in range(1, NZ):
        joined = joined + facts[step]
    own_marks[...] = joined
    for copy in place_copies:
        copy.wait()
    pick(0, emb_ref, 0, 4)
    spread(0, 0, 4)
    marks[me] = joined

    def send_marks(j, _):
        pltpu.make_async_remote_copy(
            src_ref=own_marks,
            dst_ref=marks.at[me],
            send_sem=mark_send,
            recv_sem=mark_recv,
            device_id=spot_device(lax.rem(me + j, 16)),
            device_id_type=MESH,
        ).start()
        return 0

    lax.fori_loop(1, 16, send_marks, 0)
    for load in loads:
        load.wait()

    for piece in range(4):
        for way in range(2):
            ring_copies[way, 1, piece].wait_recv()
            hop(way, 2, piece)
    pick(1, up_1, 0, 4)
    pick(2, down_1, 0, 4)
    spread(1, 0, 4)
    spread(2, 0, 4)
    most_marks = marks.at[pl.ds(0, 15)]
    pltpu.make_async_copy(most_marks, most_marks, mark_recv).wait()
    lax.fori_loop(0, 3, learn, 0)

    for piece in range(4):
        for way in range(2):
            ring_copies[way, 2, piece].wait_recv()
            if piece == 0:
                hop(way, 3, 0)
            elif piece == 1:
                for part in (1, 2, 3):
                    hop(way, 3, part)
        for way in range(2):
            join(way, 2, piece)
        if piece >= 2:
            first, last = ((0, 1), (1, 4))[piece - 2]
            for way in range(2):
                pick(3 + way, joints[way][2], first, last)
            spread(3, first, last)
            spread(4, first, last)

    for kind in range(4):
        for way in range(2):
            ring_copies[way, 3, kind].wait_recv()
            if kind == 0:
                hop(way, 4, 0)
                hop(way, 4, 1)
        for way in range(2):
            join(way, 3, kind)
            pick(5 + way, joints[way][3], kind, kind + 1)
        spread(5, kind, kind + 1)
        spread(6, kind, kind + 1)
        if kind < 2:
            lax.fori_loop(3 + kind, 4 + kind, learn, 0)

    for piece in range(2):
        for way in range(2):
            ring_copies[way, 4, piece].wait_recv()
            join(way, 4, piece)
            kind = 2 * way + piece
            pick(7, joints[way][4], kind, kind + 1)
        for way in range(2):
            kind = 2 * way + piece
            spread(7, kind, kind + 1)
    lax.fori_loop(5, 7, learn, 0)

    ours = core * half
    theirs = half - ours

    def to_partner(src, dst, i):
        copy = pltpu.make_async_remote_copy(
            src_ref=src,
            dst_ref=dst,
            send_sem=swap_send.at[i],
            recv_sem=swap_recv.at[i],
            device_id=partner,
            device_id_type=MESH,
        )
        copy.start()
        return copy

    our_half = pl.ds(pl.multiple_of(ours, 16), half)
    their_half = pl.ds(pl.multiple_of(theirs, 16), half)
    swaps = [to_partner(total.at[their_half], other, 0)]
    received(7)
    forward(7)
    swaps.append(to_partner(turned.at[their_half], turned_other, 1))
    swaps.append(to_partner(low_ref, low_other, 2))
    vec_swap = to_partner(vec_total, vec_other, 3)
    total[our_half] += jnp.dot(turned[our_half], low_ref[...], preferred_element_type=f32)

    vec_swap.wait_recv()
    vec_sum = vec_total[...] + vec_other[...]
    grad_vec = jnp.sum(vec_sum, axis=1)
    new_first_vec = beta_one * first_vec_ref[...] + (1.0 - beta_one) * grad_vec
    new_second_vec = beta_two * second_vec_ref[...] + (1.0 - beta_two) * grad_vec * grad_vec
    vector = jnp.concatenate([bias_ref[...].astype(f32), out_w_ref[...].astype(f32)], axis=0)
    new_first_vec_ref[...] = new_first_vec
    new_second_vec_ref[...] = new_second_vec
    new_vec_ref[...] = (
        vector - learn_rate * new_first_vec / (jnp.sqrt(new_second_vec) + epsilon)
    ).astype(jnp.bfloat16)

    for copy in swaps:
        copy.wait_recv()
    total[our_half] += jnp.dot(turned_other[...], low_other[...], preferred_element_type=f32)
    copies = []
    for i in range(2):

        def adam(r, _):
            here = pl.multiple_of(i * piece_rows + r * 16, 16)
            at = pl.ds(here, 16)
            there = pl.ds(pl.multiple_of(ours + here, 16), 16)
            grad = total[there] + other[at]
            first = beta_one * first_ref[at] + (1.0 - beta_one) * grad
            second = beta_two * second_ref[at] + (1.0 - beta_two) * grad * grad
            new_first[at] = first
            new_second[at] = second
            new_w[there] = (
                w_ref[there].astype(f32) - learn_rate * first / (jnp.sqrt(second) + epsilon)
            ).astype(jnp.bfloat16)
            return 0

        lax.fori_loop(0, piece_rows // 16, adam, 0, unroll=3)
        there = pl.ds(pl.multiple_of(ours + i * piece_rows, 16), piece_rows)
        copies.append(to_partner(new_w.at[there], new_w.at[there], 4 + i))

    vec_swap.wait_send()
    for copy in swaps:
        copy.wait_send()
    for copy in ring_copies.values():
        copy.wait_send()
    pltpu.make_async_copy(most_marks, most_marks, mark_send).wait()
    for step in range(NZ):
        most = got.at[step, :, pl.ds(0, 15)]
        pltpu.make_async_copy(most, most, plane_send.at[step]).wait()
    for copy in copies:
        copy.wait()


def write_kernel(*refs):
    held, placed, sem = refs[:6], refs[6:12], refs[12]
    copies = [
        pltpu.make_async_copy(src, dst, sem.at[i])
        for i, (src, dst) in enumerate(zip(held, placed, strict=True))
    ]
    for copy in copies:
        copy.start()
    for copy in copies:
        copy.wait()


def per_device(
    embeddings, coverage, labels, w_in, bias_in, w_out, first_w, second_w, first_vec, second_vec
):
    feature = embeddings.shape[2]
    hid = w_in.shape[2]
    half = feature // 2
    bf16, i32, f32 = jnp.bfloat16, jnp.int32, jnp.float32
    dma, vmem = pltpu.SemaphoreType.DMA, pltpu.VMEM
    smem_in = pl.BlockSpec(memory_space=pltpu.SMEM)
    vmem_in = pl.BlockSpec(memory_space=vmem)
    any_in = pl.BlockSpec(memory_space=pl.ANY)
    order, table_marks, table_spots = pl.pallas_call(
        plan_kernel,
        out_shape=(
            jax.ShapeDtypeStruct((2, 64), i32),
            jax.ShapeDtypeStruct((NZ, 16, 128), bf16),
            jax.ShapeDtypeStruct((NZ, 2, 128), i32),
        ),
        in_specs=[vmem_in] * 2,
        out_specs=[vmem_in] * 3,
        name="plan",
    )(coverage.T, labels.transpose(1, 2, 0))
    results = (
        ((2, hid), bf16),
        ((2, hid), f32),
        ((2, hid), f32),
        ((feature, hid), bf16),
        ((half, hid), f32),
        ((half, hid), f32),
    )
    made = pl.pallas_call(
        step_kernel,
        out_shape=[vmem(shape, kind) for shape, kind in results],
        in_specs=[smem_in, *[vmem_in] * 7, *[any_in] * 3],
        out_specs=[vmem_in] * 6,
        scratch_shapes=[
            vmem((64, 8, feature), bf16),
            vmem((64, 8, feature), bf16),
            *[vmem((size, 8, feature), bf16) for size in (64, 56, 8, 24, 8, 8, 8, 8, 8) * 2],
            *[vmem((size, 8, feature), bf16) for size in (64, 48, 16) * 2],
            vmem((NZ, 2, 16, 8, feature), bf16),
            vmem((NZ, 2, 16, 8, feature), bf16),
            vmem((NZ, 16, 128), bf16),
            vmem((NZ, 2, 128), i32),
            vmem((16, 128), bf16),
            vmem((16, 16, 128), bf16),
            vmem((feature, hid), bf16),
            vmem((half, hid), f32),
            vmem((half, hid), f32),
            vmem((256, hid), f32),
            vmem((256, hid), bf16),
            vmem((256, hid), bf16),
            vmem((feature, 256), bf16),
            vmem((half, 256), bf16),
            vmem((feature, hid), f32),
            vmem((half, hid), f32),
            vmem((2, 8, hid), f32),
            vmem((2, 8, hid), f32),
            vmem((256, 1), f32),
            pltpu.SMEM((NZ, 2, 128), i32),
            dma((2, 4, 4)),
            dma((2, 4, 4)),
            dma((2, NZ)),
            dma((2, NZ)),
            dma((NZ,)),
            dma((NZ,)),
            dma,
            dma,
            dma((NZ,)),
            dma((NZ,)),
            dma((5,)),
            dma((6,)),
            dma((6,)),
        ],
        compiler_params=pltpu.CompilerParams(
            collective_id=0, has_side_effects=True, vmem_limit_bytes=50 << 20
        ),
        name="adam_step",
    )(
        order, table_marks, table_spots, embeddings, bias_in, w_out, first_vec[0], second_vec[0],
        w_in[0], first_w[0], second_w[0],
    )
    made = [pltpu.with_memory_space_constraint(array, vmem) for array in made]
    new_vec, new_first_vec, new_second_vec, new_w, new_first, new_second = pl.pallas_call(
        write_kernel,
        out_shape=[jax.ShapeDtypeStruct(shape, kind) for shape, kind in results],
        in_specs=[vmem_in] * 6,
        out_specs=[any_in] * 6,
        scratch_shapes=[dma((6,))],
        compiler_params=pltpu.CompilerParams(vmem_limit_bytes=2 << 20),
        name="write",
    )(*made)
    return (
        new_w[None],
        new_vec[None],
        new_first[None],
        new_second[None],
        new_first_vec[None],
        new_second_vec[None],
    )


def solution(mesh):
    owners = ("dp", "head")
    moments = P(owners, "rep", None)
    vectors = P(owners, None, None)
    everyone = ("dp", "head", "rep")
    placed = (
        P(everyone, None, None),
        P(everyone, None),
        P(everyone, None, None),
        vectors,
        P(owners, None),
        P(owners, None),
        moments,
        moments,
        vectors,
        vectors,
    )
    return jax.shard_map(
        per_device,
        mesh=mesh,
        in_specs=placed,
        out_specs=(vectors, vectors, moments, moments, vectors, vectors),
        check_vma=False,
    )
```

```python
import jax
import jax.numpy as jnp
from jax import lax
from jax.experimental import pallas as pl
from jax.experimental.pallas import tpu as pltpu
from jax.sharding import PartitionSpec as P

beta_one = 0.9
beta_two = 0.999
learn_rate = 0.001
epsilon = 1e-08

MESH = pl.DeviceIdType.MESH
NZ = 8
STEP_OF = (0, 1, 3, 5, 7, 6, 4, 2)
PIECES = {
    1: ((0, 32), (32, 56), (56, 64)),
    2: ((0, 32), (32, 56), (56, 64)),
    3: ((0, 24), (24, 32), (32, 40), (40, 48)),
    4: ((0, 8), (8, 16)),
}


def plan_kernel(cover_ref, labels_ref, order_ref, marks_ref, spots_ref):
    z = lax.rem(lax.axis_index("dp"), NZ)
    f32, i32, bf16 = jnp.float32, jnp.int32, jnp.bfloat16
    blocks = 64
    square = (blocks, blocks)
    down_axis = lax.broadcasted_iota(i32, square, 0)
    along = lax.broadcasted_iota(i32, square, 1)
    number = lax.broadcasted_iota(i32, (1, blocks), 1)

    def upright(row):
        spread = jnp.where(down_axis == along, jnp.broadcast_to(row, square), 0)
        return jnp.sum(spread.astype(f32), axis=1, keepdims=True).astype(i32)

    def count(flags):
        return jnp.sum(jnp.where(flags, 1.0, 0.0), axis=0, keepdims=True).astype(i32)

    heads = [cover_ref[t : t + 1] for t in range(2)]
    ahead, spot, up, keys = [], [], [], [[], []]
    for head in heads:
        plane = (head >> 2) & 7
        x, y = head & 3, head >> 5
        kind = (x + y) & 3
        gap = (plane - z + NZ) & 7
        is_up = ((gap >= 1) & (gap <= 3)) | ((gap == 4) & (kind < 2))
        for way in range(2):
            hops = gap if way == 0 else NZ - gap
            far = (gap == 4) & (is_up if way == 0 else ~is_up)
            beyond = jnp.where(far, 10 - (kind & 1), jnp.where(hops == 3, 8 - kind, 0))
            first = jnp.where(hops == 2, 20 - kind, jnp.where(far, 10, beyond))
            keys[way].append((first, beyond))
        ahead.append(gap)
        spot.append(4 * kind + x)
        up.append(is_up)

    wide = lax.broadcasted_iota(i32, (blocks, 128), 1)
    earlier = down_axis < along
    places, thirds, orders, relays = [], [], [], []
    for way in range(2):
        first, beyond = (jnp.maximum(keys[way][0][i], keys[way][1][i]) for i in range(2))
        tall = upright(first)
        pos = count((tall > first) | ((tall == first) & earlier))
        tall_pos = upright(pos)
        order = jnp.sum(jnp.where(tall_pos == along, down_axis, 0).astype(f32), axis=0, keepdims=True)
        orders.append(order.astype(i32))
        tall = upright(beyond)
        same = count((tall == beyond) & earlier)
        more = count(tall > beyond)
        third = jnp.where(beyond >= 8, more + same, jnp.where(beyond > 0, 24 + 8 * (7 - beyond) + same, 99))
        relay = jnp.where(upright(third) == wide, tall_pos, 0).astype(f32)
        relays.append(jnp.sum(relay, axis=0, keepdims=True).astype(i32))
        places.append(pos)
        thirds.append(third)
    order_ref[0:1] = orders[0]
    order_ref[1:2] = orders[1]

    tall_heads = [upright(head) for head in heads]
    ranks = [
        count((tall_heads[0] == heads[0]) & earlier),
        count(tall_heads[0] == heads[1]) + count((tall_heads[1] == heads[1]) & earlier),
    ]
    row = lax.broadcasted_iota(i32, (8, blocks), 0)
    lanes = lax.broadcasted_iota(i32, (blocks, NZ * 128), 1)
    table = None
    for t in range(2):
        plane, gap = (heads[t] >> 2) & 7, ahead[t]
        step = jnp.where(gap < 4, jnp.maximum(2 * gap - 1, 0), jnp.where(gap == 4, 7, 2 * (NZ - gap)))
        lane = plane * 128 + step * 16 + spot[t]
        picker = jnp.where(upright(lane) == lanes, 1.0, 0.0).astype(bf16)
        far = (gap >= 3) & (gap <= 5)
        there = [jnp.where(far, thirds[way], places[way]) for way in range(2)]
        pos = jnp.where(gap == 0, number, jnp.where(up[t], there[0], there[1]))
        mark = labels_ref[t] + 1
        rank = jnp.broadcast_to(ranks[t], (8, blocks))
        tall_pos = jnp.broadcast_to(pos, (8, blocks))
        facts = jnp.concatenate(
            [
                jnp.where(rank == 0, mark, 0).astype(f32),
                jnp.where(rank == 1, mark, 0).astype(f32),
                jnp.where(rank == row, tall_pos, 0).astype(f32),
            ],
            axis=0,
        ).astype(bf16)
        part = jnp.dot(facts, picker, preferred_element_type=f32)
        table = part if table is None else table + part
    for plane in range(NZ):
        part = table[:, plane * 128 : plane * 128 + 128]
        marks_ref[plane] = part[0:16].astype(bf16)
        gap = (plane - z + NZ) & 7
        spots_ref[plane, 0:2] = part[16:18].astype(i32)
        spots_ref[plane, 2:3] = jnp.where(gap == 2, relays[0], jnp.where(gap == 6, relays[1], 0))
        spots_ref[plane, 3:4] = jnp.zeros((1, 128), i32)


def step_kernel(
    order_ref, plan_marks, plan_spots, emb_ref, bias_ref, out_w_ref, first_vec_ref, second_vec_ref,
    w_hbm, first_hbm, second_hbm,
    new_vec_ref, new_first_vec_ref, new_second_vec_ref, new_w, new_first, new_second,
    send_up, send_down,
    up_1, up_2a, up_2b, up_2c, up_3a, up_3b, up_3c, up_3d, up_4a, up_4b,
    down_1, down_2a, down_2b, down_2c, down_3a, down_3b, down_3c, down_3d, down_4a, down_4b,
    up_2, up_3, up_4, up_next, down_2, down_3, down_4, down_next,
    picked, got, facts, spots, own_marks, marks, w_ref, first_ref, second_ref,
    pre_ref, low_ref, low_other, turned, turned_other, total, other, vec_total, vec_other,
    mark_col, places,
    ring_send, ring_recv, fact_send, fact_recv, place_sem, own_sem,
    mark_send, mark_recv, plane_send, plane_recv, load_sem, swap_send, swap_recv,
):
    dp, x, core = lax.axis_index("dp"), lax.axis_index("head"), lax.axis_index("rep")
    y, z = dp // NZ, lax.rem(dp, NZ)
    me = 4 * lax.rem(x + y, 4) + x
    partner = (dp, x, 1 - core)
    feature, hid = w_ref.shape
    half = feature // 2
    piece_rows = half // 2
    f32 = jnp.float32

    def at_plane(z_to):
        return (y * NZ + z_to, x, core)

    def spot_device(p):
        x_to = lax.rem(p, 4)
        return (lax.rem(p // 4 - x_to + 4, 4) * NZ + z, x_to, core)

    barrier = pltpu.get_barrier_semaphore()
    for d in range(1, NZ):
        pl.semaphore_signal(
            barrier, inc=1, device_id=at_plane(lax.rem(z + d, NZ)), device_id_type=MESH
        )

    def greet(j, _):
        device = spot_device(lax.rem(me + j, 16))
        pl.semaphore_signal(barrier, inc=1, device_id=device, device_id_type=MESH)
        return 0

    lax.fori_loop(1, 16, greet, 0)
    pl.semaphore_signal(barrier, inc=1, device_id=partner, device_id_type=MESH)

    def arrange(i, _):
        send_up[i] = emb_ref[order_ref[0, i]]
        send_down[i] = emb_ref[order_ref[1, i]]
        return 0

    lax.fori_loop(0, 64, arrange, 0, unroll=4)
    tables = ((plan_marks, facts), (plan_spots, spots))
    own_tables = [
        pltpu.make_async_copy(table.at[z], held.at[0], load_sem.at[3 + i])
        for i, (table, held) in enumerate(tables)
    ]
    for copy in own_tables:
        copy.start()
    pl.semaphore_wait(barrier, 23)

    def parts(ref, number):
        return [ref.at[pl.ds(low, high - low)] for low, high in PIECES[number]]

    arrivals = (
        {
            1: parts(up_1, 1),
            2: (up_2a, up_2b, up_2c),
            3: (up_3a, up_3b, up_3c, up_3d),
            4: (up_4a, up_4b),
        },
        {
            1: parts(down_1, 1),
            2: (down_2a, down_2b, down_2c),
            3: (down_3a, down_3b, down_3c, down_3d),
            4: (down_4a, down_4b),
        },
    )
    sources = (
        {1: send_up, 2: up_1, 3: up_next, 4: up_3a},
        {1: send_down, 2: down_1, 3: down_next, 4: down_3a},
    )
    joints = ({2: up_2, 3: up_3, 4: up_4}, {2: down_2, 3: down_3, 4: down_4})
    targets = (at_plane(lax.rem(z + 1, NZ)), at_plane(lax.rem(z + NZ - 1, NZ)))
    ring_copies = {}

    def hop(way, number, piece):
        low, high = PIECES[number][piece]
        copy = pltpu.make_async_remote_copy(
            src_ref=sources[way][number].at[pl.ds(low, high - low)],
            dst_ref=arrivals[way][number][piece],
            send_sem=ring_send.at[way, number - 1, piece],
            recv_sem=ring_recv.at[way, number - 1, piece],
            device_id=targets[way],
            device_id_type=MESH,
        )
        copy.start()
        ring_copies[way, number, piece] = copy

    def join(way, number, piece):
        low, high = PIECES[number][piece]
        joints[way][number][pl.ds(low, high - low)] = arrivals[way][number][piece][...]

    fact_copies = []
    for d in range(1, NZ):
        z_to = lax.rem(z + d, NZ)
        for i, (table, held) in enumerate(tables):
            copy = pltpu.make_async_remote_copy(
                src_ref=table.at[z_to],
                dst_ref=held.at[STEP_OF[d]],
                send_sem=fact_send.at[i, d],
                recv_sem=fact_recv.at[i, STEP_OF[d]],
                device_id=at_plane(z_to),
                device_id_type=MESH,
            )
            copy.start()
            fact_copies.append(copy)

    for piece in range(3):
        for way in range(2):
            hop(way, 1, piece)

    loads = [
        pltpu.make_async_copy(src, dst, load_sem.at[i])
        for i, (src, dst) in enumerate(
            ((w_hbm, w_ref), (first_hbm, first_ref), (second_hbm, second_ref))
        )
    ]
    for load in loads:
        load.start()

    def pick(step, source, first, last):
        def one(p, _):
            for k in range(2):
                picked[step, k, p] = source[places[step, k, step * 16 + p]]
            return 0

        lax.fori_loop(4 * first, 4 * last, one, 0, unroll=4)

    def spread(step, first, last):
        def send(j, _):
            p = (j // 4) * 4 + lax.rem(x + j, 4)

            @pl.when(p != me)
            def _():
                pltpu.make_async_remote_copy(
                    src_ref=picked.at[step, :, p],
                    dst_ref=got.at[step, :, me],
                    send_sem=plane_send.at[step],
                    recv_sem=plane_recv.at[step],
                    device_id=spot_device(p),
                    device_id_type=MESH,
                ).start()

            @pl.when(p == me)
            def _():
                pltpu.make_async_copy(
                    picked.at[step, :, me], got.at[step, :, me], own_sem.at[step]
                ).start()

            return 0

        lax.fori_loop(4 * first, 4 * last, send, 0)

    def received(step):
        most = got.at[step, :, pl.ds(0, 15)]
        pltpu.make_async_copy(most, most, plane_recv.at[step]).wait()
        pltpu.make_async_copy(picked.at[step, :, me], got.at[step, :, me], own_sem.at[step]).wait()

    def forward(step):
        rows = got[step].reshape(256, feature)
        turned[...] = rows.T
        pre_ref[...] = jnp.dot(rows, w_ref[...], preferred_element_type=f32) + bias_ref[...].astype(f32)
        lanes = lax.broadcasted_iota(jnp.int32, (128, 128), 1)
        every = marks[...].astype(f32)
        for k in range(2):
            mine = every[:, 8 * k : 8 * k + 8].reshape(128, 128)
            mine = jnp.where(lanes == me + 16 * step, mine, 0.0)
            mark_col[pl.ds(128 * k, 128)] = jnp.sum(mine, axis=1, keepdims=True)

        out_w = out_w_ref[...].astype(f32)

        def group(i, _):
            at = pl.ds(pl.multiple_of(i * 16, 16), 16)
            pre = pre_ref[at]
            mark = mark_col[at]
            sig = 1.0 / (1.0 + jnp.exp(-pre))
            hidden = pre * sig
            logits = jnp.sum(hidden * out_w, axis=1, keepdims=True)
            guess = 1.0 / (1.0 + jnp.exp(-logits))
            residual = jnp.where(mark > 0.5, guess - (mark - 1.0), 0.0)
            grad_pre = residual * out_w * sig * (1.0 + pre * (1.0 - sig))
            low_ref[at] = grad_pre.astype(jnp.bfloat16)
            vec_total[0] += grad_pre[0:8] + grad_pre[8:16]
            swing = residual * hidden
            vec_total[1] += swing[0:8] + swing[8:16]
            return 0

        lax.fori_loop(0, 16, group, 0, unroll=4)

    def learn(step, _):
        received(step)
        forward(step)
        for i in range(2):
            at = pl.ds(i * half, half)
            total[at] += jnp.dot(turned[at], low_ref[...], preferred_element_type=f32)
        return 0

    total[...] = jnp.zeros_like(total)
    vec_total[...] = jnp.zeros_like(vec_total)

    for copy in fact_copies:
        copy.wait()
    for copy in own_tables:
        copy.wait()
    place_copies = []
    for step in range(NZ):
        copy = pltpu.make_async_copy(
            spots.at[step], places.at[step], place_sem.at[step]
        )
        copy.start()
        place_copies.append(copy)
    joined = facts[0]
    for step in range(1, NZ):
        joined = joined + facts[step]
    own_marks[...] = joined
    for copy in place_copies:
        copy.wait()
    pick(0, emb_ref, 0, 4)
    spread(0, 0, 4)
    marks[me] = joined

    def send_marks(j, _):
        pltpu.make_async_remote_copy(
            src_ref=own_marks,
            dst_ref=marks.at[me],
            send_sem=mark_send,
            recv_sem=mark_recv,
            device_id=spot_device(lax.rem(me + j, 16)),
            device_id_type=MESH,
        ).start()
        return 0

    lax.fori_loop(1, 16, send_marks, 0)
    for load in loads:
        load.wait()

    def relay(way, low, high):
        def one(i, _):
            sources[way][3][i] = joints[way][2][places[3 + way, 2, i]]
            return 0

        lax.fori_loop(low, high, one, 0, unroll=4)

    for piece in range(3):
        for way in range(2):
            ring_copies[way, 1, piece].wait_recv()
            hop(way, 2, piece)
    pick(1, up_1, 0, 4)
    pick(2, down_1, 0, 4)
    spread(1, 0, 4)
    spread(2, 0, 4)
    most_marks = marks.at[pl.ds(0, 15)]
    pltpu.make_async_copy(most_marks, most_marks, mark_recv).wait()
    lax.fori_loop(0, 1, learn, 0)

    for way, source in enumerate((up_2a, down_2a)):
        ring_copies[way, 2, 0].wait_recv()
        pick(3 + way, source, 0, 4)
    spread(3, 0, 4)
    spread(4, 0, 4)
    for way in range(2):
        join(way, 2, 0)
    lax.fori_loop(1, 2, learn, 0)

    for way in range(2):
        ring_copies[way, 2, 1].wait_recv()
        join(way, 2, 1)
        relay(way, 0, 24)
    for way in range(2):
        hop(way, 3, 0)
    for way in range(2):
        ring_copies[way, 2, 2].wait_recv()
        join(way, 2, 2)
        relay(way, 24, 48)
    for way in range(2):
        for piece in (1, 2, 3):
            hop(way, 3, piece)
    lax.fori_loop(2, 5, learn, 0)

    for kind in range(4):
        for way in range(2):
            ring_copies[way, 3, kind].wait_recv()
            if kind == 0:
                hop(way, 4, 0)
                hop(way, 4, 1)
        for way in range(2):
            join(way, 3, kind)
            pick(5 + way, joints[way][3], kind, kind + 1)
        spread(5, kind, kind + 1)
        spread(6, kind, kind + 1)

    for piece in range(2):
        for way in range(2):
            ring_copies[way, 4, piece].wait_recv()
            join(way, 4, piece)
            kind = 2 * way + piece
            pick(7, joints[way][4], kind, kind + 1)
        for way in range(2):
            kind = 2 * way + piece
            spread(7, kind, kind + 1)
    lax.fori_loop(5, 7, learn, 0)

    ours = core * half
    theirs = half - ours

    def to_partner(src, dst, i):
        copy = pltpu.make_async_remote_copy(
            src_ref=src,
            dst_ref=dst,
            send_sem=swap_send.at[i],
            recv_sem=swap_recv.at[i],
            device_id=partner,
            device_id_type=MESH,
        )
        copy.start()
        return copy

    our_half = pl.ds(pl.multiple_of(ours, 16), half)
    their_half = pl.ds(pl.multiple_of(theirs, 16), half)
    swaps = [to_partner(total.at[their_half], other, 0)]
    received(7)
    forward(7)
    swaps.append(to_partner(turned.at[their_half], turned_other, 1))
    swaps.append(to_partner(low_ref, low_other, 2))
    vec_swap = to_partner(vec_total, vec_other, 3)
    total[our_half] += jnp.dot(turned[our_half], low_ref[...], preferred_element_type=f32)

    vec_swap.wait_recv()
    vec_sum = vec_total[...] + vec_other[...]
    grad_vec = jnp.sum(vec_sum, axis=1)
    new_first_vec = beta_one * first_vec_ref[...] + (1.0 - beta_one) * grad_vec
    new_second_vec = beta_two * second_vec_ref[...] + (1.0 - beta_two) * grad_vec * grad_vec
    vector = jnp.concatenate([bias_ref[...].astype(f32), out_w_ref[...].astype(f32)], axis=0)
    new_first_vec_ref[...] = new_first_vec
    new_second_vec_ref[...] = new_second_vec
    new_vec_ref[...] = (
        vector - learn_rate * new_first_vec / (jnp.sqrt(new_second_vec) + epsilon)
    ).astype(jnp.bfloat16)

    for copy in swaps:
        copy.wait_recv()
    total[our_half] += jnp.dot(turned_other[...], low_other[...], preferred_element_type=f32)
    copies = []
    for i in range(2):

        def adam(r, _):
            here = pl.multiple_of(i * piece_rows + r * 16, 16)
            at = pl.ds(here, 16)
            there = pl.ds(pl.multiple_of(ours + here, 16), 16)
            grad = total[there] + other[at]
            first = beta_one * first_ref[at] + (1.0 - beta_one) * grad
            second = beta_two * second_ref[at] + (1.0 - beta_two) * grad * grad
            new_first[at] = first
            new_second[at] = second
            new_w[there] = (
                w_ref[there].astype(f32) - learn_rate * first / (jnp.sqrt(second) + epsilon)
            ).astype(jnp.bfloat16)
            return 0

        lax.fori_loop(0, piece_rows // 16, adam, 0, unroll=3)
        there = pl.ds(pl.multiple_of(ours + i * piece_rows, 16), piece_rows)
        copies.append(to_partner(new_w.at[there], new_w.at[there], 4 + i))

    vec_swap.wait_send()
    for copy in swaps:
        copy.wait_send()
    for copy in ring_copies.values():
        copy.wait_send()
    pltpu.make_async_copy(most_marks, most_marks, mark_send).wait()
    for step in range(NZ):
        most = got.at[step, :, pl.ds(0, 15)]
        pltpu.make_async_copy(most, most, plane_send.at[step]).wait()
    for copy in copies:
        copy.wait()


def write_kernel(*refs):
    held, placed, sem = refs[:6], refs[6:12], refs[12]
    copies = [
        pltpu.make_async_copy(src, dst, sem.at[i])
        for i, (src, dst) in enumerate(zip(held, placed, strict=True))
    ]
    for copy in copies:
        copy.start()
    for copy in copies:
        copy.wait()


def per_device(
    embeddings, coverage, labels, w_in, bias_in, w_out, first_w, second_w, first_vec, second_vec
):
    feature = embeddings.shape[2]
    hid = w_in.shape[2]
    half = feature // 2
    bf16, i32, f32 = jnp.bfloat16, jnp.int32, jnp.float32
    dma, vmem = pltpu.SemaphoreType.DMA, pltpu.VMEM
    smem_in = pl.BlockSpec(memory_space=pltpu.SMEM)
    vmem_in = pl.BlockSpec(memory_space=vmem)
    any_in = pl.BlockSpec(memory_space=pl.ANY)
    order, table_marks, table_spots = pl.pallas_call(
        plan_kernel,
        out_shape=(
            jax.ShapeDtypeStruct((2, 64), i32),
            jax.ShapeDtypeStruct((NZ, 16, 128), bf16),
            jax.ShapeDtypeStruct((NZ, 4, 128), i32),
        ),
        in_specs=[vmem_in] * 2,
        out_specs=[vmem_in] * 3,
        name="plan",
    )(coverage.T, labels.transpose(1, 2, 0))
    results = (
        ((2, hid), bf16),
        ((2, hid), f32),
        ((2, hid), f32),
        ((feature, hid), bf16),
        ((half, hid), f32),
        ((half, hid), f32),
    )
    made = pl.pallas_call(
        step_kernel,
        out_shape=[vmem(shape, kind) for shape, kind in results],
        in_specs=[smem_in, *[vmem_in] * 7, *[any_in] * 3],
        out_specs=[vmem_in] * 6,
        scratch_shapes=[
            vmem((64, 8, feature), bf16),
            vmem((64, 8, feature), bf16),
            *[vmem((size, 8, feature), bf16) for size in (64, 32, 24, 8, 24, 8, 8, 8, 8, 8) * 2],
            *[vmem((size, 8, feature), bf16) for size in (64, 48, 16, 48) * 2],
            vmem((NZ, 2, 16, 8, feature), bf16),
            vmem((NZ, 2, 16, 8, feature), bf16),
            vmem((NZ, 16, 128), bf16),
            vmem((NZ, 4, 128), i32),
            vmem((16, 128), bf16),
            vmem((16, 16, 128), bf16),
            vmem((feature, hid), bf16),
            vmem((half, hid), f32),
            vmem((half, hid), f32),
            vmem((256, hid), f32),
            vmem((256, hid), bf16),
            vmem((256, hid), bf16),
            vmem((feature, 256), bf16),
            vmem((half, 256), bf16),
            vmem((feature, hid), f32),
            vmem((half, hid), f32),
            vmem((2, 8, hid), f32),
            vmem((2, 8, hid), f32),
            vmem((256, 1), f32),
            pltpu.SMEM((NZ, 4, 128), i32),
            dma((2, 4, 4)),
            dma((2, 4, 4)),
            dma((2, NZ)),
            dma((2, NZ)),
            dma((NZ,)),
            dma((NZ,)),
            dma,
            dma,
            dma((NZ,)),
            dma((NZ,)),
            dma((5,)),
            dma((6,)),
            dma((6,)),
        ],
        compiler_params=pltpu.CompilerParams(
            collective_id=0, has_side_effects=True, vmem_limit_bytes=50 << 20
        ),
        name="adam_step",
    )(
        order, table_marks, table_spots, embeddings, bias_in, w_out, first_vec[0], second_vec[0],
        w_in[0], first_w[0], second_w[0],
    )
    made = [pltpu.with_memory_space_constraint(array, vmem) for array in made]
    new_vec, new_first_vec, new_second_vec, new_w, new_first, new_second = pl.pallas_call(
        write_kernel,
        out_shape=[jax.ShapeDtypeStruct(shape, kind) for shape, kind in results],
        in_specs=[vmem_in] * 6,
        out_specs=[any_in] * 6,
        scratch_shapes=[dma((6,))],
        compiler_params=pltpu.CompilerParams(vmem_limit_bytes=2 << 20),
        name="write",
    )(*made)
    return (
        new_w[None],
        new_vec[None],
        new_first[None],
        new_second[None],
        new_first_vec[None],
        new_second_vec[None],
    )


def solution(mesh):
    owners = ("dp", "head")
    moments = P(owners, "rep", None)
    vectors = P(owners, None, None)
    everyone = ("dp", "head", "rep")
    placed = (
        P(everyone, None, None),
        P(everyone, None),
        P(everyone, None, None),
        vectors,
        P(owners, None),
        P(owners, None),
        moments,
        moments,
        vectors,
        vectors,
    )
    return jax.shard_map(
        per_device,
        mesh=mesh,
        in_specs=placed,
        out_specs=(vectors, vectors, moments, moments, vectors, vectors),
        check_vma=False,
    )
```

```python
import jax
import jax.numpy as jnp
from jax import lax
from jax.experimental import pallas as pl
from jax.experimental.pallas import tpu as pltpu
from jax.sharding import PartitionSpec as P

beta_one = 0.9
beta_two = 0.999
learn_rate = 0.001
epsilon = 1e-08

MESH = pl.DeviceIdType.MESH
NZ = 8
STEP_OF = (0, 1, 3, 5, 7, 6, 4, 2)
PIECES = {
    1: ((0, 32), (32, 56), (56, 64)),
    2: ((0, 32), (32, 56), (56, 64)),
    3: ((0, 24), (24, 32), (32, 40), (40, 48)),
    4: ((0, 8), (8, 16)),
}


def plan_kernel(cover_ref, labels_ref, order_ref, marks_ref, spots_ref):
    z = lax.rem(lax.axis_index("dp"), NZ)
    f32, i32, bf16 = jnp.float32, jnp.int32, jnp.bfloat16
    blocks = 64
    square = (blocks, blocks)
    down_axis = lax.broadcasted_iota(i32, square, 0)
    along = lax.broadcasted_iota(i32, square, 1)
    number = lax.broadcasted_iota(i32, (1, blocks), 1)

    def upright(row):
        spread = jnp.where(down_axis == along, jnp.broadcast_to(row, square), 0)
        return jnp.sum(spread.astype(f32), axis=1, keepdims=True).astype(i32)

    def count(flags):
        return jnp.sum(jnp.where(flags, 1.0, 0.0), axis=0, keepdims=True).astype(i32)

    heads = [cover_ref[t : t + 1] for t in range(2)]
    ahead, spot, up, keys = [], [], [], [[], []]
    for head in heads:
        plane = (head >> 2) & 7
        x, y = head & 3, head >> 5
        kind = (x + y) & 3
        gap = (plane - z + NZ) & 7
        is_up = ((gap >= 1) & (gap <= 3)) | ((gap == 4) & (kind < 2))
        for way in range(2):
            hops = gap if way == 0 else NZ - gap
            far = (gap == 4) & (is_up if way == 0 else ~is_up)
            beyond = jnp.where(far, 10 - (kind & 1), jnp.where(hops == 3, 8 - kind, 0))
            first = jnp.where(hops == 2, 20 - kind, jnp.where(far, 10, beyond))
            keys[way].append((first, beyond))
        ahead.append(gap)
        spot.append(4 * kind + x)
        up.append(is_up)

    wide = lax.broadcasted_iota(i32, (blocks, 128), 1)
    earlier = down_axis < along
    places, thirds, orders, relays = [], [], [], []
    for way in range(2):
        first, beyond = (jnp.maximum(keys[way][0][i], keys[way][1][i]) for i in range(2))
        tall = upright(first)
        pos = count((tall > first) | ((tall == first) & earlier))
        tall_pos = upright(pos)
        order = jnp.sum(jnp.where(tall_pos == along, down_axis, 0).astype(f32), axis=0, keepdims=True)
        orders.append(order.astype(i32))
        tall = upright(beyond)
        same = count((tall == beyond) & earlier)
        more = count(tall > beyond)
        third = jnp.where(beyond >= 8, more + same, jnp.where(beyond > 0, 24 + 8 * (7 - beyond) + same, 99))
        relay = jnp.where(upright(third) == wide, tall_pos, 0).astype(f32)
        relays.append(jnp.sum(relay, axis=0, keepdims=True).astype(i32))
        places.append(pos)
        thirds.append(third)
    order_ref[0:1] = orders[0]
    order_ref[1:2] = orders[1]

    tall_heads = [upright(head) for head in heads]
    ranks = [
        count((tall_heads[0] == heads[0]) & earlier),
        count(tall_heads[0] == heads[1]) + count((tall_heads[1] == heads[1]) & earlier),
    ]
    row = lax.broadcasted_iota(i32, (8, blocks), 0)
    lanes = lax.broadcasted_iota(i32, (blocks, NZ * 128), 1)
    table = None
    for t in range(2):
        plane, gap = (heads[t] >> 2) & 7, ahead[t]
        step = jnp.where(gap < 4, jnp.maximum(2 * gap - 1, 0), jnp.where(gap == 4, 7, 2 * (NZ - gap)))
        lane = plane * 128 + step * 16 + spot[t]
        picker = jnp.where(upright(lane) == lanes, 1.0, 0.0).astype(bf16)
        far = (gap >= 3) & (gap <= 5)
        there = [jnp.where(far, thirds[way], places[way]) for way in range(2)]
        pos = jnp.where(gap == 0, number, jnp.where(up[t], there[0], there[1]))
        mark = labels_ref[t] + 1
        rank = jnp.broadcast_to(ranks[t], (8, blocks))
        tall_pos = jnp.broadcast_to(pos, (8, blocks))
        facts = jnp.concatenate(
            [
                jnp.where(rank == 0, mark, 0).astype(f32),
                jnp.where(rank == 1, mark, 0).astype(f32),
                jnp.where(rank == row, tall_pos, 0).astype(f32),
            ],
            axis=0,
        ).astype(bf16)
        part = jnp.dot(facts, picker, preferred_element_type=f32)
        table = part if table is None else table + part
    for plane in range(NZ):
        part = table[:, plane * 128 : plane * 128 + 128]
        marks_ref[plane] = part[0:16].astype(bf16)
        gap = (plane - z + NZ) & 7
        spots_ref[plane, 0:2] = part[16:18].astype(i32)
        spots_ref[plane, 2:3] = jnp.where(gap == 2, relays[0], jnp.where(gap == 6, relays[1], 0))
        spots_ref[plane, 3:4] = jnp.zeros((1, 128), i32)


def step_kernel(
    order_ref, plan_marks, plan_spots, emb_hbm, bias_ref, out_w_ref, first_vec_ref, second_vec_ref,
    w_hbm, first_hbm, second_hbm,
    new_vec_ref, new_first_vec_ref, new_second_vec_ref, new_w, new_first, new_second,
    emb_ref, send_up, send_down,
    up_1, up_2a, up_2b, up_2c, up_3a, up_3b, up_3c, up_3d, up_4a, up_4b,
    down_1, down_2a, down_2b, down_2c, down_3a, down_3b, down_3c, down_3d, down_4a, down_4b,
    up_2, up_3, up_4, up_next, down_2, down_3, down_4, down_next,
    picked, got, facts, spots, own_marks, marks, w_ref, first_ref, second_ref,
    pre_ref, low_ref, low_other, turned, turned_other, total, other, vec_total, vec_other,
    mark_col, places,
    ring_send, ring_recv, fact_send, fact_recv, place_sem, own_sem,
    mark_send, mark_recv, plane_send, plane_recv, load_sem, swap_send, swap_recv,
):
    dp, x, core = lax.axis_index("dp"), lax.axis_index("head"), lax.axis_index("rep")
    y, z = dp // NZ, lax.rem(dp, NZ)
    me = 4 * lax.rem(x + y, 4) + x
    partner = (dp, x, 1 - core)
    feature, hid = w_ref.shape
    half = feature // 2
    piece_rows = half // 2
    f32 = jnp.float32

    def at_plane(z_to):
        return (y * NZ + z_to, x, core)

    def spot_device(p):
        x_to = lax.rem(p, 4)
        return (lax.rem(p // 4 - x_to + 4, 4) * NZ + z, x_to, core)

    barrier = pltpu.get_barrier_semaphore()
    for d in range(1, NZ):
        pl.semaphore_signal(
            barrier, inc=1, device_id=at_plane(lax.rem(z + d, NZ)), device_id_type=MESH
        )

    def greet(j, _):
        device = spot_device(lax.rem(me + j, 16))
        pl.semaphore_signal(barrier, inc=1, device_id=device, device_id_type=MESH)
        return 0

    lax.fori_loop(1, 16, greet, 0)
    pl.semaphore_signal(barrier, inc=1, device_id=partner, device_id_type=MESH)

    emb_copy = pltpu.make_async_copy(emb_hbm, emb_ref, load_sem.at[5])
    emb_copy.start()
    emb_copy.wait()

    def arrange(i, _):
        send_up[i] = emb_ref[order_ref[0, i]]
        send_down[i] = emb_ref[order_ref[1, i]]
        return 0

    lax.fori_loop(0, 64, arrange, 0, unroll=4)
    tables = ((plan_marks, facts), (plan_spots, spots))
    own_tables = [
        pltpu.make_async_copy(table.at[z], held.at[0], load_sem.at[3 + i])
        for i, (table, held) in enumerate(tables)
    ]
    for copy in own_tables:
        copy.start()
    pl.semaphore_wait(barrier, 23)

    def parts(ref, number):
        return [ref.at[pl.ds(low, high - low)] for low, high in PIECES[number]]

    arrivals = (
        {
            1: parts(up_1, 1),
            2: (up_2a, up_2b, up_2c),
            3: (up_3a, up_3b, up_3c, up_3d),
            4: (up_4a, up_4b),
        },
        {
            1: parts(down_1, 1),
            2: (down_2a, down_2b, down_2c),
            3: (down_3a, down_3b, down_3c, down_3d),
            4: (down_4a, down_4b),
        },
    )
    sources = (
        {1: send_up, 2: up_1, 3: up_next, 4: up_3a},
        {1: send_down, 2: down_1, 3: down_next, 4: down_3a},
    )
    joints = ({2: up_2, 3: up_3, 4: up_4}, {2: down_2, 3: down_3, 4: down_4})
    targets = (at_plane(lax.rem(z + 1, NZ)), at_plane(lax.rem(z + NZ - 1, NZ)))
    ring_copies = {}

    def hop(way, number, piece):
        low, high = PIECES[number][piece]
        copy = pltpu.make_async_remote_copy(
            src_ref=sources[way][number].at[pl.ds(low, high - low)],
            dst_ref=arrivals[way][number][piece],
            send_sem=ring_send.at[way, number - 1, piece],
            recv_sem=ring_recv.at[way, number - 1, piece],
            device_id=targets[way],
            device_id_type=MESH,
        )
        copy.start()
        ring_copies[way, number, piece] = copy

    def join(way, number, piece):
        low, high = PIECES[number][piece]
        joints[way][number][pl.ds(low, high - low)] = arrivals[way][number][piece][...]

    fact_copies = []
    for d in range(1, NZ):
        z_to = lax.rem(z + d, NZ)
        for i, (table, held) in enumerate(tables):
            copy = pltpu.make_async_remote_copy(
                src_ref=table.at[z_to],
                dst_ref=held.at[STEP_OF[d]],
                send_sem=fact_send.at[i, d],
                recv_sem=fact_recv.at[i, STEP_OF[d]],
                device_id=at_plane(z_to),
                device_id_type=MESH,
            )
            copy.start()
            fact_copies.append(copy)

    for way in range(2):
        hop(way, 1, 0)

    def gone(way, number, piece):
        ring_copies[way, number, piece].wait_send()
        left.add((way, number, piece))

    left = set()
    loads = [
        pltpu.make_async_copy(src, dst, load_sem.at[i])
        for i, (src, dst) in enumerate(
            ((w_hbm, w_ref), (first_hbm, first_ref), (second_hbm, second_ref))
        )
    ]
    for load in loads:
        load.start()

    def pick(step, source, first, last):
        def one(p, _):
            for k in range(2):
                picked[step, k, p] = source[places[step, k, step * 16 + p]]
            return 0

        lax.fori_loop(4 * first, 4 * last, one, 0, unroll=4)

    def spread(step, first, last):
        def send(j, _):
            p = (j // 4) * 4 + lax.rem(x + j, 4)

            @pl.when(p != me)
            def _():
                pltpu.make_async_remote_copy(
                    src_ref=picked.at[step, :, p],
                    dst_ref=got.at[step, :, me],
                    send_sem=plane_send.at[step],
                    recv_sem=plane_recv.at[step],
                    device_id=spot_device(p),
                    device_id_type=MESH,
                ).start()

            @pl.when(p == me)
            def _():
                pltpu.make_async_copy(
                    picked.at[step, :, me], got.at[step, :, me], own_sem.at[step]
                ).start()

            return 0

        lax.fori_loop(4 * first, 4 * last, send, 0)

    def sent(step):
        most = got.at[step, :, pl.ds(0, 15)]
        pltpu.make_async_copy(most, most, plane_send.at[step]).wait()

    def received(step):
        most = got.at[step, :, pl.ds(0, 15)]
        pltpu.make_async_copy(most, most, plane_recv.at[step]).wait()
        pltpu.make_async_copy(picked.at[step, :, me], got.at[step, :, me], own_sem.at[step]).wait()

    def forward(step):
        rows = got[step].reshape(256, feature)
        turned[...] = rows.T
        pre_ref[...] = jnp.dot(rows, w_ref[...], preferred_element_type=f32) + bias_ref[...].astype(f32)
        lanes = lax.broadcasted_iota(jnp.int32, (128, 128), 1)
        every = marks[...].astype(f32)
        for k in range(2):
            mine = every[:, 8 * k : 8 * k + 8].reshape(128, 128)
            mine = jnp.where(lanes == me + 16 * step, mine, 0.0)
            mark_col[pl.ds(128 * k, 128)] = jnp.sum(mine, axis=1, keepdims=True)

        out_w = out_w_ref[...].astype(f32)

        def group(i, _):
            at = pl.ds(pl.multiple_of(i * 16, 16), 16)
            pre = pre_ref[at]
            mark = mark_col[at]
            sig = 1.0 / (1.0 + jnp.exp(-pre))
            hidden = pre * sig
            logits = jnp.sum(hidden * out_w, axis=1, keepdims=True)
            guess = 1.0 / (1.0 + jnp.exp(-logits))
            residual = jnp.where(mark > 0.5, guess - (mark - 1.0), 0.0)
            grad_pre = residual * out_w * sig * (1.0 + pre * (1.0 - sig))
            low_ref[at] = grad_pre.astype(jnp.bfloat16)
            vec_total[0] += grad_pre[0:8] + grad_pre[8:16]
            swing = residual * hidden
            vec_total[1] += swing[0:8] + swing[8:16]
            return 0

        lax.fori_loop(0, 16, group, 0, unroll=8)

    def learn(step, _):
        received(step)
        forward(step)
        for i in range(2):
            at = pl.ds(i * half, half)
            total[at] += jnp.dot(turned[at], low_ref[...], preferred_element_type=f32)
        return 0

    total[...] = jnp.zeros_like(total)
    vec_total[...] = jnp.zeros_like(vec_total)

    for copy in fact_copies:
        copy.wait()
    for copy in own_tables:
        copy.wait()
    place_copies = []
    for step in range(NZ):
        copy = pltpu.make_async_copy(
            spots.at[step], places.at[step], place_sem.at[step]
        )
        copy.start()
        place_copies.append(copy)
    joined = facts[0]
    for step in range(1, NZ):
        joined = joined + facts[step]
    own_marks[...] = joined
    for copy in place_copies:
        copy.wait()
    pick(0, emb_ref, 0, 4)
    spread(0, 0, 4)
    marks[me] = joined

    def send_marks(j, _):
        pltpu.make_async_remote_copy(
            src_ref=own_marks,
            dst_ref=marks.at[me],
            send_sem=mark_send,
            recv_sem=mark_recv,
            device_id=spot_device(lax.rem(me + j, 16)),
            device_id_type=MESH,
        ).start()
        return 0

    lax.fori_loop(1, 16, send_marks, 0)
    for load in loads:
        load.wait()

    def relay(way, low, high):
        def one(i, _):
            sources[way][3][i] = joints[way][2][places[3 + way, 2, i]]
            return 0

        lax.fori_loop(low, high, one, 0, unroll=4)

    for way in range(2):
        gone(way, 1, 0)
        hop(way, 1, 1)
    for way in range(2):
        ring_copies[way, 1, 0].wait_recv()
        gone(way, 1, 1)
        hop(way, 1, 2)
        hop(way, 2, 0)
    for way, source in enumerate((up_1, down_1)):
        for piece in (1, 2):
            ring_copies[way, 1, piece].wait_recv()
        pick(1 + way, source, 0, 4)
    spread(1, 0, 4)
    spread(2, 0, 4)
    most_marks = marks.at[pl.ds(0, 15)]
    pltpu.make_async_copy(most_marks, most_marks, mark_recv).wait()
    lax.fori_loop(0, 1, learn, 0)

    for way in range(2):
        gone(way, 2, 0)
        hop(way, 2, 1)
    for way, source in enumerate((up_2a, down_2a)):
        ring_copies[way, 2, 0].wait_recv()
        pick(3 + way, source, 0, 4)
    spread(3, 0, 4)
    spread(4, 0, 4)
    for way in range(2):
        join(way, 2, 0)
    for way in range(2):
        gone(way, 2, 1)
        hop(way, 2, 2)
    for way in range(2):
        ring_copies[way, 2, 1].wait_recv()
        join(way, 2, 1)
        relay(way, 0, 24)
    for way in range(2):
        hop(way, 3, 0)
    for way in range(2):
        ring_copies[way, 2, 2].wait_recv()
        join(way, 2, 2)
        relay(way, 24, 48)
    lax.fori_loop(1, 3, learn, 0)

    for way in range(2):
        gone(way, 3, 0)
        hop(way, 3, 1)
    for kind in range(4):
        for way in range(2):
            ring_copies[way, 3, kind].wait_recv()
            join(way, 3, kind)
            pick(5 + way, joints[way][3], kind, kind + 1)
        if kind == 0:
            for way in range(2):
                hop(way, 3, 2)
        spread(5, kind, kind + 1)
        spread(6, kind, kind + 1)
        if kind == 0:
            lax.fori_loop(3, 4, learn, 0)
        if kind < 3:
            number, piece = ((3, 3), (4, 0), (4, 1))[kind]
            for way in range(2):
                gone(way, 3, kind + 1)
                hop(way, number, piece)
        if kind == 2:
            lax.fori_loop(4, 5, learn, 0)

    for piece in range(2):
        for way in range(2):
            ring_copies[way, 4, piece].wait_recv()
            join(way, 4, piece)
            kind = 2 * way + piece
            pick(7, joints[way][4], kind, kind + 1)
        if piece == 0:
            sent(5)
            sent(6)
        for way in range(2):
            kind = 2 * way + piece
            spread(7, kind, kind + 1)
    lax.fori_loop(5, 7, learn, 0)

    ours = core * half
    theirs = half - ours

    def to_partner(src, dst, i):
        copy = pltpu.make_async_remote_copy(
            src_ref=src,
            dst_ref=dst,
            send_sem=swap_send.at[i],
            recv_sem=swap_recv.at[i],
            device_id=partner,
            device_id_type=MESH,
        )
        copy.start()
        return copy

    our_half = pl.ds(pl.multiple_of(ours, 16), half)
    their_half = pl.ds(pl.multiple_of(theirs, 16), half)
    swaps = [to_partner(total.at[their_half], other, 0)]
    received(7)
    forward(7)
    swaps.append(to_partner(turned.at[their_half], turned_other, 1))
    swaps.append(to_partner(low_ref, low_other, 2))
    vec_swap = to_partner(vec_total, vec_other, 3)
    total[our_half] += jnp.dot(turned[our_half], low_ref[...], preferred_element_type=f32)

    vec_swap.wait_recv()
    vec_sum = vec_total[...] + vec_other[...]
    grad_vec = jnp.sum(vec_sum, axis=1)
    new_first_vec = beta_one * first_vec_ref[...] + (1.0 - beta_one) * grad_vec
    new_second_vec = beta_two * second_vec_ref[...] + (1.0 - beta_two) * grad_vec * grad_vec
    vector = jnp.concatenate([bias_ref[...].astype(f32), out_w_ref[...].astype(f32)], axis=0)
    new_first_vec_ref[...] = new_first_vec
    new_second_vec_ref[...] = new_second_vec
    new_vec_ref[...] = (
        vector - learn_rate * new_first_vec / (jnp.sqrt(new_second_vec) + epsilon)
    ).astype(jnp.bfloat16)

    for copy in swaps:
        copy.wait_recv()
    total[our_half] += jnp.dot(turned_other[...], low_other[...], preferred_element_type=f32)
    copies = []
    for i in range(2):

        def adam(r, _):
            here = pl.multiple_of(i * piece_rows + r * 16, 16)
            at = pl.ds(here, 16)
            there = pl.ds(pl.multiple_of(ours + here, 16), 16)
            grad = total[there] + other[at]
            first = beta_one * first_ref[at] + (1.0 - beta_one) * grad
            second = beta_two * second_ref[at] + (1.0 - beta_two) * grad * grad
            new_first[at] = first
            new_second[at] = second
            new_w[there] = (
                w_ref[there].astype(f32) - learn_rate * first / (jnp.sqrt(second) + epsilon)
            ).astype(jnp.bfloat16)
            return 0

        lax.fori_loop(0, piece_rows // 16, adam, 0, unroll=3)
        there = pl.ds(pl.multiple_of(ours + i * piece_rows, 16), piece_rows)
        copies.append(to_partner(new_w.at[there], new_w.at[there], 4 + i))

    vec_swap.wait_send()
    for copy in swaps:
        copy.wait_send()
    for key, copy in ring_copies.items():
        if key not in left:
            copy.wait_send()
    pltpu.make_async_copy(most_marks, most_marks, mark_send).wait()
    for step in (0, 1, 2, 3, 4, 7):
        sent(step)
    for copy in copies:
        copy.wait()


def write_kernel(*refs):
    held, placed, sem = refs[:6], refs[6:12], refs[12]
    copies = [
        pltpu.make_async_copy(src, dst, sem.at[i])
        for i, (src, dst) in enumerate(zip(held, placed, strict=True))
    ]
    for copy in copies:
        copy.start()
    for copy in copies:
        copy.wait()


def per_device(
    embeddings, coverage, labels, w_in, bias_in, w_out, first_w, second_w, first_vec, second_vec
):
    feature = embeddings.shape[2]
    hid = w_in.shape[2]
    half = feature // 2
    bf16, i32, f32 = jnp.bfloat16, jnp.int32, jnp.float32
    dma, vmem = pltpu.SemaphoreType.DMA, pltpu.VMEM
    smem_in = pl.BlockSpec(memory_space=pltpu.SMEM)
    vmem_in = pl.BlockSpec(memory_space=vmem)
    any_in = pl.BlockSpec(memory_space=pl.ANY)
    order, table_marks, table_spots = pl.pallas_call(
        plan_kernel,
        out_shape=(
            jax.ShapeDtypeStruct((2, 64), i32),
            jax.ShapeDtypeStruct((NZ, 16, 128), bf16),
            jax.ShapeDtypeStruct((NZ, 4, 128), i32),
        ),
        in_specs=[vmem_in] * 2,
        out_specs=[vmem_in] * 3,
        name="plan",
    )(coverage.T, labels.transpose(1, 2, 0))
    results = (
        ((2, hid), bf16),
        ((2, hid), f32),
        ((2, hid), f32),
        ((feature, hid), bf16),
        ((half, hid), f32),
        ((half, hid), f32),
    )
    made = pl.pallas_call(
        step_kernel,
        out_shape=[vmem(shape, kind) for shape, kind in results],
        in_specs=[smem_in, *[vmem_in] * 2, any_in, *[vmem_in] * 4, *[any_in] * 3],
        out_specs=[vmem_in] * 6,
        scratch_shapes=[
            *[vmem((64, 8, feature), bf16) for _ in range(3)],
            *[vmem((size, 8, feature), bf16) for size in (64, 32, 24, 8, 24, 8, 8, 8, 8, 8) * 2],
            *[vmem((size, 8, feature), bf16) for size in (64, 48, 16, 48) * 2],
            vmem((NZ, 2, 16, 8, feature), bf16),
            vmem((NZ, 2, 16, 8, feature), bf16),
            vmem((NZ, 16, 128), bf16),
            vmem((NZ, 4, 128), i32),
            vmem((16, 128), bf16),
            vmem((16, 16, 128), bf16),
            vmem((feature, hid), bf16),
            vmem((half, hid), f32),
            vmem((half, hid), f32),
            vmem((256, hid), f32),
            vmem((256, hid), bf16),
            vmem((256, hid), bf16),
            vmem((feature, 256), bf16),
            vmem((half, 256), bf16),
            vmem((feature, hid), f32),
            vmem((half, hid), f32),
            vmem((2, 8, hid), f32),
            vmem((2, 8, hid), f32),
            vmem((256, 1), f32),
            pltpu.SMEM((NZ, 4, 128), i32),
            dma((2, 4, 4)),
            dma((2, 4, 4)),
            dma((2, NZ)),
            dma((2, NZ)),
            dma((NZ,)),
            dma((NZ,)),
            dma,
            dma,
            dma((NZ,)),
            dma((NZ,)),
            dma((6,)),
            dma((6,)),
            dma((6,)),
        ],
        compiler_params=pltpu.CompilerParams(
            collective_id=0, has_side_effects=True, vmem_limit_bytes=50 << 20
        ),
        name="adam_step",
    )(
        order, table_marks, table_spots, embeddings, bias_in, w_out, first_vec[0], second_vec[0],
        w_in[0], first_w[0], second_w[0],
    )
    made = [pltpu.with_memory_space_constraint(array, vmem) for array in made]
    new_vec, new_first_vec, new_second_vec, new_w, new_first, new_second = pl.pallas_call(
        write_kernel,
        out_shape=[jax.ShapeDtypeStruct(shape, kind) for shape, kind in results],
        in_specs=[vmem_in] * 6,
        out_specs=[any_in] * 6,
        scratch_shapes=[dma((6,))],
        compiler_params=pltpu.CompilerParams(vmem_limit_bytes=2 << 20),
        name="write",
    )(*made)
    return (
        new_w[None],
        new_vec[None],
        new_first[None],
        new_second[None],
        new_first_vec[None],
        new_second_vec[None],
    )


def solution(mesh):
    owners = ("dp", "head")
    moments = P(owners, "rep", None)
    vectors = P(owners, None, None)
    everyone = ("dp", "head", "rep")
    placed = (
        P(everyone, None, None),
        P(everyone, None),
        P(everyone, None, None),
        vectors,
        P(owners, None),
        P(owners, None),
        moments,
        moments,
        vectors,
        vectors,
    )
    return jax.shard_map(
        per_device,
        mesh=mesh,
        in_specs=placed,
        out_specs=(vectors, vectors, moments, moments, vectors, vectors),
        check_vma=False,
    )
```

```python
import jax
import jax.numpy as jnp
from jax import lax
from jax.experimental import pallas as pl
from jax.experimental.pallas import tpu as pltpu
from jax.sharding import PartitionSpec as P

beta_one = 0.9
beta_two = 0.999
learn_rate = 0.001
epsilon = 1e-08

MESH = pl.DeviceIdType.MESH
NZ = 8
STEP_OF = (0, 1, 3, 5, 7, 6, 4, 2)
PIECES = {
    1: ((0, 32), (32, 56), (56, 64)),
    2: ((0, 32), (32, 56), (56, 64)),
    3: ((0, 24), (24, 32), (32, 40), (40, 48)),
    4: ((0, 8), (8, 16)),
}


def plan_kernel(cover_ref, labels_ref, order_ref, marks_ref, spots_ref):
    z = lax.rem(lax.axis_index("dp"), NZ)
    f32, i32, bf16 = jnp.float32, jnp.int32, jnp.bfloat16
    blocks = 64
    square = (blocks, blocks)
    down_axis = lax.broadcasted_iota(i32, square, 0)
    along = lax.broadcasted_iota(i32, square, 1)
    number = lax.broadcasted_iota(i32, (1, blocks), 1)

    def upright(row):
        spread = jnp.where(down_axis == along, jnp.broadcast_to(row, square), 0)
        return jnp.sum(spread.astype(f32), axis=1, keepdims=True).astype(i32)

    def count(flags):
        return jnp.sum(jnp.where(flags, 1.0, 0.0), axis=0, keepdims=True).astype(i32)

    heads = [cover_ref[t : t + 1] for t in range(2)]
    ahead, spot, up, keys = [], [], [], [[], []]
    for head in heads:
        plane = (head >> 2) & 7
        x, y = head & 3, head >> 5
        kind = (x + y) & 3
        gap = (plane - z + NZ) & 7
        is_up = ((gap >= 1) & (gap <= 3)) | ((gap == 4) & (kind < 2))
        for way in range(2):
            hops = gap if way == 0 else NZ - gap
            far = (gap == 4) & (is_up if way == 0 else ~is_up)
            beyond = jnp.where(far, 10 - (kind & 1), jnp.where(hops == 3, 8 - kind, 0))
            first = jnp.where(hops == 2, 20 - kind, jnp.where(far, 10, beyond))
            keys[way].append((first, beyond))
        ahead.append(gap)
        spot.append(4 * kind + x)
        up.append(is_up)

    wide = lax.broadcasted_iota(i32, (blocks, 128), 1)
    earlier = down_axis < along
    places, thirds, orders, relays = [], [], [], []
    for way in range(2):
        first, beyond = (jnp.maximum(keys[way][0][i], keys[way][1][i]) for i in range(2))
        tall = upright(first)
        pos = count((tall > first) | ((tall == first) & earlier))
        tall_pos = upright(pos)
        order = jnp.sum(jnp.where(tall_pos == along, down_axis, 0).astype(f32), axis=0, keepdims=True)
        orders.append(order.astype(i32))
        tall = upright(beyond)
        same = count((tall == beyond) & earlier)
        more = count(tall > beyond)
        third = jnp.where(beyond >= 8, more + same, jnp.where(beyond > 0, 24 + 8 * (7 - beyond) + same, 99))
        relay = jnp.where(upright(third) == wide, tall_pos, 0).astype(f32)
        relays.append(jnp.sum(relay, axis=0, keepdims=True).astype(i32))
        places.append(pos)
        thirds.append(third)
    order_ref[0:1] = orders[0]
    order_ref[1:2] = orders[1]

    tall_heads = [upright(head) for head in heads]
    ranks = [
        count((tall_heads[0] == heads[0]) & earlier),
        count(tall_heads[0] == heads[1]) + count((tall_heads[1] == heads[1]) & earlier),
    ]
    row = lax.broadcasted_iota(i32, (8, blocks), 0)
    lanes = lax.broadcasted_iota(i32, (blocks, NZ * 128), 1)
    table = None
    for t in range(2):
        plane, gap = (heads[t] >> 2) & 7, ahead[t]
        step = jnp.where(gap < 4, jnp.maximum(2 * gap - 1, 0), jnp.where(gap == 4, 7, 2 * (NZ - gap)))
        lane = plane * 128 + step * 16 + spot[t]
        picker = jnp.where(upright(lane) == lanes, 1.0, 0.0).astype(bf16)
        far = (gap >= 3) & (gap <= 5)
        there = [jnp.where(far, thirds[way], places[way]) for way in range(2)]
        pos = jnp.where(gap == 0, number, jnp.where(up[t], there[0], there[1]))
        mark = labels_ref[t] + 1
        rank = jnp.broadcast_to(ranks[t], (8, blocks))
        tall_pos = jnp.broadcast_to(pos, (8, blocks))
        facts = jnp.concatenate(
            [
                jnp.where(rank == 0, mark, 0).astype(f32),
                jnp.where(rank == 1, mark, 0).astype(f32),
                jnp.where(rank == row, tall_pos, 0).astype(f32),
            ],
            axis=0,
        ).astype(bf16)
        part = jnp.dot(facts, picker, preferred_element_type=f32)
        table = part if table is None else table + part
    for plane in range(NZ):
        part = table[:, plane * 128 : plane * 128 + 128]
        marks_ref[plane] = part[0:16].astype(bf16)
        gap = (plane - z + NZ) & 7
        spots_ref[plane, 0:2] = part[16:18].astype(i32)
        spots_ref[plane, 2:3] = jnp.where(gap == 2, relays[0], jnp.where(gap == 6, relays[1], 0))
        spots_ref[plane, 3:4] = jnp.zeros((1, 128), i32)


def step_kernel(
    order_ref, plan_marks, plan_spots, emb_hbm, bias_ref, out_w_ref, first_vec_ref, second_vec_ref,
    w_hbm, first_hbm, second_hbm,
    new_vec_ref, new_first_vec_ref, new_second_vec_ref, new_w, new_first, new_second,
    emb_ref, send_up, send_down,
    up_1, up_2a, up_2b, up_2c, up_3a, up_3b, up_3c, up_3d, up_4a, up_4b,
    down_1, down_2a, down_2b, down_2c, down_3a, down_3b, down_3c, down_3d, down_4a, down_4b,
    up_2, up_3, up_4, up_next, down_2, down_3, down_4, down_next,
    picked, got, facts, spots, own_marks, marks, w_ref, first_ref, second_ref,
    pre_ref, low_ref, low_pair, low_other, turned, turned_pair, turned_other, total, other, vec_total, vec_other,
    mark_col, places,
    ring_send, ring_recv, fact_send, fact_recv, place_sem, own_sem,
    mark_send, mark_recv, plane_send, plane_recv, load_sem, swap_send, swap_recv,
):
    dp, x, core = lax.axis_index("dp"), lax.axis_index("head"), lax.axis_index("rep")
    y, z = dp // NZ, lax.rem(dp, NZ)
    me = 4 * lax.rem(x + y, 4) + x
    partner = (dp, x, 1 - core)
    feature, hid = w_ref.shape
    half = feature // 2
    piece_rows = half // 2
    f32 = jnp.float32

    def at_plane(z_to):
        return (y * NZ + z_to, x, core)

    def spot_device(p):
        x_to = lax.rem(p, 4)
        return (lax.rem(p // 4 - x_to + 4, 4) * NZ + z, x_to, core)

    barrier = pltpu.get_barrier_semaphore()
    for d in range(1, NZ):
        pl.semaphore_signal(
            barrier, inc=1, device_id=at_plane(lax.rem(z + d, NZ)), device_id_type=MESH
        )

    def greet(j, _):
        device = spot_device(lax.rem(me + j, 16))
        pl.semaphore_signal(barrier, inc=1, device_id=device, device_id_type=MESH)
        return 0

    lax.fori_loop(1, 16, greet, 0)
    pl.semaphore_signal(barrier, inc=1, device_id=partner, device_id_type=MESH)

    emb_copy = pltpu.make_async_copy(emb_hbm, emb_ref, load_sem.at[5])
    emb_copy.start()
    emb_copy.wait()

    def arrange(i, _):
        send_up[i] = emb_ref[order_ref[0, i]]
        send_down[i] = emb_ref[order_ref[1, i]]
        return 0

    lax.fori_loop(0, 64, arrange, 0, unroll=4)
    tables = ((plan_marks, facts), (plan_spots, spots))
    own_tables = [
        pltpu.make_async_copy(table.at[z], held.at[0], load_sem.at[3 + i])
        for i, (table, held) in enumerate(tables)
    ]
    for copy in own_tables:
        copy.start()
    pl.semaphore_wait(barrier, 23)

    def parts(ref, number):
        return [ref.at[pl.ds(low, high - low)] for low, high in PIECES[number]]

    arrivals = (
        {
            1: parts(up_1, 1),
            2: (up_2a, up_2b, up_2c),
            3: (up_3a, up_3b, up_3c, up_3d),
            4: (up_4a, up_4b),
        },
        {
            1: parts(down_1, 1),
            2: (down_2a, down_2b, down_2c),
            3: (down_3a, down_3b, down_3c, down_3d),
            4: (down_4a, down_4b),
        },
    )
    sources = (
        {1: send_up, 2: up_1, 3: up_next, 4: up_3a},
        {1: send_down, 2: down_1, 3: down_next, 4: down_3a},
    )
    joints = ({2: up_2, 3: up_3, 4: up_4}, {2: down_2, 3: down_3, 4: down_4})
    targets = (at_plane(lax.rem(z + 1, NZ)), at_plane(lax.rem(z + NZ - 1, NZ)))
    ring_copies = {}

    def hop(way, number, piece):
        low, high = PIECES[number][piece]
        copy = pltpu.make_async_remote_copy(
            src_ref=sources[way][number].at[pl.ds(low, high - low)],
            dst_ref=arrivals[way][number][piece],
            send_sem=ring_send.at[way, number - 1, piece],
            recv_sem=ring_recv.at[way, number - 1, piece],
            device_id=targets[way],
            device_id_type=MESH,
        )
        copy.start()
        ring_copies[way, number, piece] = copy

    def join(way, number, piece):
        low, high = PIECES[number][piece]
        joints[way][number][pl.ds(low, high - low)] = arrivals[way][number][piece][...]

    fact_copies = []
    for d in range(1, NZ):
        z_to = lax.rem(z + d, NZ)
        for i, (table, held) in enumerate(tables):
            copy = pltpu.make_async_remote_copy(
                src_ref=table.at[z_to],
                dst_ref=held.at[STEP_OF[d]],
                send_sem=fact_send.at[i, d],
                recv_sem=fact_recv.at[i, STEP_OF[d]],
                device_id=at_plane(z_to),
                device_id_type=MESH,
            )
            copy.start()
            fact_copies.append(copy)

    for way in range(2):
        hop(way, 1, 0)

    def gone(way, number, piece):
        ring_copies[way, number, piece].wait_send()
        left.add((way, number, piece))

    left = set()
    loads = [
        pltpu.make_async_copy(src, dst, load_sem.at[i])
        for i, (src, dst) in enumerate(
            ((w_hbm, w_ref), (first_hbm, first_ref), (second_hbm, second_ref))
        )
    ]
    for load in loads:
        load.start()

    def pick(step, source, first, last):
        def one(p, _):
            for k in range(2):
                picked[step, k, p] = source[places[step, k, step * 16 + p]]
            return 0

        lax.fori_loop(4 * first, 4 * last, one, 0, unroll=4)

    def spread(step, first, last):
        def send(j, _):
            p = (j // 4) * 4 + lax.rem(x + j, 4)

            @pl.when(p != me)
            def _():
                pltpu.make_async_remote_copy(
                    src_ref=picked.at[step, :, p],
                    dst_ref=got.at[step, :, me],
                    send_sem=plane_send.at[step],
                    recv_sem=plane_recv.at[step],
                    device_id=spot_device(p),
                    device_id_type=MESH,
                ).start()

            @pl.when(p == me)
            def _():
                pltpu.make_async_copy(
                    picked.at[step, :, me], got.at[step, :, me], own_sem.at[step]
                ).start()

            return 0

        lax.fori_loop(4 * first, 4 * last, send, 0)

    def sent(step):
        most = got.at[step, :, pl.ds(0, 15)]
        pltpu.make_async_copy(most, most, plane_send.at[step]).wait()

    def received(step):
        most = got.at[step, :, pl.ds(0, 15)]
        pltpu.make_async_copy(most, most, plane_recv.at[step]).wait()
        pltpu.make_async_copy(picked.at[step, :, me], got.at[step, :, me], own_sem.at[step]).wait()

    def forward(step, turned, low_ref, pair=1):
        rows = got[pl.ds(step, pair)].reshape(256 * pair, feature)
        turned[...] = rows.T
        pre_ref[pl.ds(0, 256 * pair)] = jnp.dot(rows, w_ref[...], preferred_element_type=f32) + bias_ref[...].astype(f32)
        lanes = lax.broadcasted_iota(jnp.int32, (128, 128), 1)
        every = marks[...].astype(f32)
        for i in range(2 * pair):
            k = i % 2
            mine = every[:, 8 * k : 8 * k + 8].reshape(128, 128)
            mine = jnp.where(lanes == me + 16 * (step + i // 2), mine, 0.0)
            mark_col[pl.ds(128 * i, 128)] = jnp.sum(mine, axis=1, keepdims=True)

        out_w = out_w_ref[...].astype(f32)

        def group(i, _):
            at = pl.ds(pl.multiple_of(i * 16, 16), 16)
            pre = pre_ref[at]
            mark = mark_col[at]
            sig = 1.0 / (1.0 + jnp.exp(-pre))
            hidden = pre * sig
            logits = jnp.sum(hidden * out_w, axis=1, keepdims=True)
            guess = 1.0 / (1.0 + jnp.exp(-logits))
            residual = jnp.where(mark > 0.5, guess - (mark - 1.0), 0.0)
            grad_pre = residual * out_w * sig * (1.0 + pre * (1.0 - sig))
            low_ref[at] = grad_pre.astype(jnp.bfloat16)
            vec_total[0] += grad_pre[0:8] + grad_pre[8:16]
            swing = residual * hidden
            vec_total[1] += swing[0:8] + swing[8:16]
            return 0

        lax.fori_loop(0, 16 * pair, group, 0, unroll=8)

    def learn(step, _):
        received(step)
        forward(step, turned, low_ref)
        for i in range(2):
            at = pl.ds(i * half, half)
            total[at] += jnp.dot(turned[at], low_ref[...], preferred_element_type=f32)
        return 0

    total[...] = jnp.zeros_like(total)
    vec_total[...] = jnp.zeros_like(vec_total)

    for copy in fact_copies:
        copy.wait()
    for copy in own_tables:
        copy.wait()
    place_copies = []
    for step in range(NZ):
        copy = pltpu.make_async_copy(
            spots.at[step], places.at[step], place_sem.at[step]
        )
        copy.start()
        place_copies.append(copy)
    joined = facts[0]
    for step in range(1, NZ):
        joined = joined + facts[step]
    own_marks[...] = joined
    for copy in place_copies:
        copy.wait()
    pick(0, emb_ref, 0, 4)
    spread(0, 0, 4)
    marks[me] = joined

    def send_marks(j, _):
        pltpu.make_async_remote_copy(
            src_ref=own_marks,
            dst_ref=marks.at[me],
            send_sem=mark_send,
            recv_sem=mark_recv,
            device_id=spot_device(lax.rem(me + j, 16)),
            device_id_type=MESH,
        ).start()
        return 0

    lax.fori_loop(1, 16, send_marks, 0)
    for load in loads:
        load.wait()

    def relay(way, low, high):
        def one(i, _):
            sources[way][3][i] = joints[way][2][places[3 + way, 2, i]]
            return 0

        lax.fori_loop(low, high, one, 0, unroll=4)

    for way in range(2):
        gone(way, 1, 0)
        hop(way, 1, 1)
    for way in range(2):
        ring_copies[way, 1, 0].wait_recv()
        gone(way, 1, 1)
        hop(way, 1, 2)
        hop(way, 2, 0)
    for way, source in enumerate((up_1, down_1)):
        for piece in (1, 2):
            ring_copies[way, 1, piece].wait_recv()
        pick(1 + way, source, 0, 4)
    spread(1, 0, 4)
    spread(2, 0, 4)
    most_marks = marks.at[pl.ds(0, 15)]
    pltpu.make_async_copy(most_marks, most_marks, mark_recv).wait()
    lax.fori_loop(0, 1, learn, 0)

    for way in range(2):
        gone(way, 2, 0)
        hop(way, 2, 1)
    for way, source in enumerate((up_2a, down_2a)):
        ring_copies[way, 2, 0].wait_recv()
        pick(3 + way, source, 0, 4)
    spread(3, 0, 4)
    spread(4, 0, 4)
    for way in range(2):
        join(way, 2, 0)
    for way in range(2):
        gone(way, 2, 1)
        hop(way, 2, 2)
    for way in range(2):
        ring_copies[way, 2, 1].wait_recv()
        join(way, 2, 1)
        relay(way, 0, 24)
    for way in range(2):
        hop(way, 3, 0)
    for way in range(2):
        ring_copies[way, 2, 2].wait_recv()
        join(way, 2, 2)
        relay(way, 24, 48)
    lax.fori_loop(1, 3, learn, 0)

    for way in range(2):
        gone(way, 3, 0)
        hop(way, 3, 1)
    for kind in range(4):
        for way in range(2):
            ring_copies[way, 3, kind].wait_recv()
            join(way, 3, kind)
            pick(5 + way, joints[way][3], kind, kind + 1)
        if kind == 0:
            for way in range(2):
                hop(way, 3, 2)
        spread(5, kind, kind + 1)
        spread(6, kind, kind + 1)
        if kind == 0:
            lax.fori_loop(3, 4, learn, 0)
        if kind < 3:
            number, piece = ((3, 3), (4, 0), (4, 1))[kind]
            for way in range(2):
                gone(way, 3, kind + 1)
                hop(way, number, piece)
        if kind == 2:
            lax.fori_loop(4, 5, learn, 0)

    for piece in range(2):
        for way in range(2):
            ring_copies[way, 4, piece].wait_recv()
            join(way, 4, piece)
            kind = 2 * way + piece
            pick(7, joints[way][4], kind, kind + 1)
        if piece == 0:
            sent(5)
            sent(6)
        for way in range(2):
            kind = 2 * way + piece
            spread(7, kind, kind + 1)
    received(5)
    received(6)
    forward(5, turned_pair, low_pair, 2)

    ours = core * half
    theirs = half - ours

    def to_partner(src, dst, i):
        copy = pltpu.make_async_remote_copy(
            src_ref=src,
            dst_ref=dst,
            send_sem=swap_send.at[i],
            recv_sem=swap_recv.at[i],
            device_id=partner,
            device_id_type=MESH,
        )
        copy.start()
        return copy

    our_half = pl.ds(pl.multiple_of(ours, 16), half)
    their_half = pl.ds(pl.multiple_of(theirs, 16), half)
    for at in (their_half, our_half):
        total[at] += jnp.dot(turned_pair[at], low_pair[...], preferred_element_type=f32)
        if at is their_half:
            swaps = [to_partner(total.at[their_half], other, 0)]
    received(7)
    forward(7, turned, low_ref)
    swaps.append(to_partner(turned.at[their_half], turned_other, 1))
    swaps.append(to_partner(low_ref, low_other, 2))
    vec_swap = to_partner(vec_total, vec_other, 3)
    total[our_half] += jnp.dot(turned[our_half], low_ref[...], preferred_element_type=f32)

    vec_swap.wait_recv()
    vec_sum = vec_total[...] + vec_other[...]
    grad_vec = jnp.sum(vec_sum, axis=1)
    new_first_vec = beta_one * first_vec_ref[...] + (1.0 - beta_one) * grad_vec
    new_second_vec = beta_two * second_vec_ref[...] + (1.0 - beta_two) * grad_vec * grad_vec
    vector = jnp.concatenate([bias_ref[...].astype(f32), out_w_ref[...].astype(f32)], axis=0)
    new_first_vec_ref[...] = new_first_vec
    new_second_vec_ref[...] = new_second_vec
    new_vec_ref[...] = (
        vector - learn_rate * new_first_vec / (jnp.sqrt(new_second_vec) + epsilon)
    ).astype(jnp.bfloat16)

    for copy in swaps:
        copy.wait_recv()
    total[our_half] += jnp.dot(turned_other[...], low_other[...], preferred_element_type=f32)
    copies = []
    for i in range(2):

        def adam(r, _):
            here = pl.multiple_of(i * piece_rows + r * 16, 16)
            at = pl.ds(here, 16)
            there = pl.ds(pl.multiple_of(ours + here, 16), 16)
            grad = total[there] + other[at]
            first = beta_one * first_ref[at] + (1.0 - beta_one) * grad
            second = beta_two * second_ref[at] + (1.0 - beta_two) * grad * grad
            new_first[at] = first
            new_second[at] = second
            new_w[there] = (
                w_ref[there].astype(f32) - learn_rate * first / (jnp.sqrt(second) + epsilon)
            ).astype(jnp.bfloat16)
            return 0

        lax.fori_loop(0, piece_rows // 16, adam, 0, unroll=3)
        there = pl.ds(pl.multiple_of(ours + i * piece_rows, 16), piece_rows)
        copies.append(to_partner(new_w.at[there], new_w.at[there], 4 + i))

    vec_swap.wait_send()
    for copy in swaps:
        copy.wait_send()
    for key, copy in ring_copies.items():
        if key not in left:
            copy.wait_send()
    pltpu.make_async_copy(most_marks, most_marks, mark_send).wait()
    for step in (0, 1, 2, 3, 4, 7):
        sent(step)
    for copy in copies:
        copy.wait()


def write_kernel(*refs):
    held, placed, sem = refs[:6], refs[6:12], refs[12]
    copies = [
        pltpu.make_async_copy(src, dst, sem.at[i])
        for i, (src, dst) in enumerate(zip(held, placed, strict=True))
    ]
    for copy in copies:
        copy.start()
    for copy in copies:
        copy.wait()


def per_device(
    embeddings, coverage, labels, w_in, bias_in, w_out, first_w, second_w, first_vec, second_vec
):
    feature = embeddings.shape[2]
    hid = w_in.shape[2]
    half = feature // 2
    bf16, i32, f32 = jnp.bfloat16, jnp.int32, jnp.float32
    dma, vmem = pltpu.SemaphoreType.DMA, pltpu.VMEM
    smem_in = pl.BlockSpec(memory_space=pltpu.SMEM)
    vmem_in = pl.BlockSpec(memory_space=vmem)
    any_in = pl.BlockSpec(memory_space=pl.ANY)
    order, table_marks, table_spots = pl.pallas_call(
        plan_kernel,
        out_shape=(
            jax.ShapeDtypeStruct((2, 64), i32),
            jax.ShapeDtypeStruct((NZ, 16, 128), bf16),
            jax.ShapeDtypeStruct((NZ, 4, 128), i32),
        ),
        in_specs=[vmem_in] * 2,
        out_specs=[vmem_in] * 3,
        name="plan",
    )(coverage.T, labels.transpose(1, 2, 0))
    results = (
        ((2, hid), bf16),
        ((2, hid), f32),
        ((2, hid), f32),
        ((feature, hid), bf16),
        ((half, hid), f32),
        ((half, hid), f32),
    )
    made = pl.pallas_call(
        step_kernel,
        out_shape=[vmem(shape, kind) for shape, kind in results],
        in_specs=[smem_in, *[vmem_in] * 2, any_in, *[vmem_in] * 4, *[any_in] * 3],
        out_specs=[vmem_in] * 6,
        scratch_shapes=[
            *[vmem((64, 8, feature), bf16) for _ in range(3)],
            *[vmem((size, 8, feature), bf16) for size in (64, 32, 24, 8, 24, 8, 8, 8, 8, 8) * 2],
            *[vmem((size, 8, feature), bf16) for size in (64, 48, 16, 48) * 2],
            vmem((NZ, 2, 16, 8, feature), bf16),
            vmem((NZ, 2, 16, 8, feature), bf16),
            vmem((NZ, 16, 128), bf16),
            vmem((NZ, 4, 128), i32),
            vmem((16, 128), bf16),
            vmem((16, 16, 128), bf16),
            vmem((feature, hid), bf16),
            vmem((half, hid), f32),
            vmem((half, hid), f32),
            vmem((512, hid), f32),
            vmem((256, hid), bf16),
            vmem((512, hid), bf16),
            vmem((256, hid), bf16),
            vmem((feature, 256), bf16),
            vmem((feature, 512), bf16),
            vmem((half, 256), bf16),
            vmem((feature, hid), f32),
            vmem((half, hid), f32),
            vmem((2, 8, hid), f32),
            vmem((2, 8, hid), f32),
            vmem((512, 1), f32),
            pltpu.SMEM((NZ, 4, 128), i32),
            dma((2, 4, 4)),
            dma((2, 4, 4)),
            dma((2, NZ)),
            dma((2, NZ)),
            dma((NZ,)),
            dma((NZ,)),
            dma,
            dma,
            dma((NZ,)),
            dma((NZ,)),
            dma((6,)),
            dma((6,)),
            dma((6,)),
        ],
        compiler_params=pltpu.CompilerParams(
            collective_id=0, has_side_effects=True, vmem_limit_bytes=50 << 20
        ),
        name="adam_step",
    )(
        order, table_marks, table_spots, embeddings, bias_in, w_out, first_vec[0], second_vec[0],
        w_in[0], first_w[0], second_w[0],
    )
    made = [pltpu.with_memory_space_constraint(array, vmem) for array in made]
    new_vec, new_first_vec, new_second_vec, new_w, new_first, new_second = pl.pallas_call(
        write_kernel,
        out_shape=[jax.ShapeDtypeStruct(shape, kind) for shape, kind in results],
        in_specs=[vmem_in] * 6,
        out_specs=[any_in] * 6,
        scratch_shapes=[dma((6,))],
        compiler_params=pltpu.CompilerParams(vmem_limit_bytes=2 << 20),
        name="write",
    )(*made)
    return (
        new_w[None],
        new_vec[None],
        new_first[None],
        new_second[None],
        new_first_vec[None],
        new_second_vec[None],
    )


def solution(mesh):
    owners = ("dp", "head")
    moments = P(owners, "rep", None)
    vectors = P(owners, None, None)
    everyone = ("dp", "head", "rep")
    placed = (
        P(everyone, None, None),
        P(everyone, None),
        P(everyone, None, None),
        vectors,
        P(owners, None),
        P(owners, None),
        moments,
        moments,
        vectors,
        vectors,
    )
    return jax.shard_map(
        per_device,
        mesh=mesh,
        in_specs=placed,
        out_specs=(vectors, vectors, moments, moments, vectors, vectors),
        check_vma=False,
    )
```
